256 devices in a mesh: seq: 64 (over y, z, core), dp: 4 (over x).
Axes of the slice: x: 4, y: 4, z: 8, core: 2. Of those that a mesh axis runs over, the one named last changes fastest.
Arguments:
- probe_vectors: bfloat16 [4, 8192, 2048], P('dp', 'seq'), may hold values from -6 to 6
- lookup_vectors: bfloat16 [4, 8192, 2048], P('dp', 'seq'), may hold values from -6 to 6
- content_vectors: bfloat16 [4, 8192, 2048], P('dp', 'seq'), may hold values from -6 to 6
- result_cotangent: bfloat16 [4, 8192, 2048], P('dp', 'seq'), may hold values from -25 to 25
- logit_softness: float32 [16], replicated, may hold values from 0.7 to 1.2
- block_grouping: int32 [4, 16, 64, 1], P('dp'), may hold values from 0 to 7, as said below
- neighborhood_span: int32 [16], replicated, may hold values from 32 to 128
Outputs:
- query_grad: bfloat16 [4, 8192, 2048], P('dp', 'seq')
- key_grad: bfloat16 [4, 8192, 2048], P('dp', 'seq')
- value_grad: bfloat16 [4, 8192, 2048], P('dp', 'seq')
- temper_grad: float32 [16], replicated
The draws below stay inside these ranges and needn't reach their ends.
Inputs may be any that keep to these rules, and one draw needn't show every extreme that they name: `block_grouping`: within one document and head no cluster holds more than 12 blocks, and some cluster holds exactly 12. Index j of seq owns the clusters c of head h with (h * 8 + c) // 2 == j; of the 1 block of one index of seq, at most 1 have for one head clusters owned by one index of seq, and that many is reached.
All inputs are finite; a program needn't handle non-finite values.
Results may differ from the reference program's by a relative error of at most 0.0076.
Values may be sent and summed in bfloat16 or wider, within the bound.
A program may use at most 64 MiB of HBM per device.

```python
import math
import jax
import jax.numpy as jnp
from jax import lax

ATTENTION_SPLITS = 16
HD = 128
BLK = 128
CORPUS_SIZE = 4
SEQLEN = 8192
NBLK = 64
NC = 8
MOST = 12
OWN = 2


def noise_field(key, label):
    field_shape = (CORPUS_SIZE, SEQLEN, ATTENTION_SPLITS * HD)
    subkey = jax.random.fold_in(key, label)
    return jnp.clip(jax.random.normal(subkey, field_shape, jnp.float32), -4.5, 4.5)


def rising(key):
    position = lax.broadcasted_iota(jnp.int32, (1, SEQLEN, 1), 1).astype(jnp.float32)
    factor = 1.0 + 2.0 * position / (SEQLEN - 1)
    return factor


def draw_probe_vectors(key, part):
    field = noise_field(key, 1)
    return field.astype(jnp.bfloat16)


def draw_lookup_vectors(key, part):
    field = noise_field(key, 2)
    return field.astype(jnp.bfloat16)


def draw_content_vectors(key, part):
    field = 0.6 * noise_field(key, 2) + 0.8 * noise_field(key, 3)
    return jnp.clip(field, -6.0, 6.0).astype(jnp.bfloat16)


def draw_result_cotangent(key, part):
    field = (0.5 * noise_field(key, 1) + 0.85 * noise_field(key, 4)) * rising(key)
    return jnp.clip(field, -25.0, 25.0).astype(jnp.bfloat16)


def draw_block_grouping(key, part):
    group_total = NC // OWN
    block_index = lax.broadcasted_iota(jnp.int32, (CORPUS_SIZE, ATTENTION_SPLITS, NBLK), 2)
    first = jax.random.randint(jax.random.fold_in(key, 11), (CORPUS_SIZE, ATTENTION_SPLITS, NBLK), 0, 1 << 20) * NBLK + block_index
    runs = first.reshape(CORPUS_SIZE, ATTENTION_SPLITS, NBLK // group_total, group_total)
    group_of = jnp.sum((runs[..., None, :] < runs[..., :, None]).astype(jnp.int32), axis=-1).reshape(CORPUS_SIZE, ATTENTION_SPLITS, NBLK)
    second = jax.random.randint(jax.random.fold_in(key, 12), (CORPUS_SIZE, ATTENTION_SPLITS, NBLK), 0, 1 << 20) * NBLK + block_index
    same_group = group_of[..., None, :] == group_of[..., :, None]
    order = jnp.sum((same_group & (second[..., None, :] < second[..., :, None])).astype(jnp.int32), axis=-1)
    forced_all = jax.random.randint(jax.random.fold_in(key, 13), (CORPUS_SIZE, ATTENTION_SPLITS, group_total), 0, OWN)
    forced = jnp.take_along_axis(forced_all, group_of, axis=2)
    rest = (forced + 1 + jnp.maximum(order - MOST, 0) % (OWN - 1)) % OWN
    local_window_part = jnp.where(order < MOST, forced, rest)
    return (group_of * OWN + local_window_part)[..., None].astype(jnp.int32)


def place_ends(result, own_key, smallest, largest):
    dims = result.shape
    place = [jax.random.randint(jax.random.fold_in(own_key, axis), (), 0, dims[axis]) for axis in range(len(dims))]
    result = result.at[tuple(place)].set(smallest)
    longest = dims.index(max(dims))
    place[longest] = (place[longest] + 1) % dims[longest]
    return result.at[tuple(place)].set(largest)


def setup_inputs(seed: int = 0) -> dict:
    arg_keys = jax.random.split(jax.random.key(seed), 8)
    return {
        "probe_vectors": draw_probe_vectors(jax.random.fold_in(arg_keys[7], 71), 0),
        "lookup_vectors": draw_lookup_vectors(jax.random.fold_in(arg_keys[7], 71), 0),
        "content_vectors": draw_content_vectors(jax.random.fold_in(arg_keys[7], 71), 0),
        "result_cotangent": draw_result_cotangent(jax.random.fold_in(arg_keys[7], 71), 0),
        "logit_softness": jnp.clip(jnp.exp(jax.random.uniform(arg_keys[4], (ATTENTION_SPLITS,), jnp.float32, math.log(0.7), math.log(1.2))), 0.7, 1.2),
        "block_grouping": draw_block_grouping(jax.random.fold_in(arg_keys[7], 71), 0),
        "neighborhood_span": place_ends(jax.random.randint(arg_keys[6], (ATTENTION_SPLITS,), BLK // 4, BLK + 1), jax.random.fold_in(arg_keys[6], 1), BLK // 4, BLK).astype(jnp.int32),
    }


blocked_score = -1e+30

def lifted(array_in):
    return lax.optimization_barrier(array_in.astype(jnp.bfloat16)).astype(jnp.float32)

def window_parts(query_block, prev_keys, prev_values, grad_block, usable, window_width, temper):
    inverse_root = 1.0 / math.sqrt(HD)
    raw_scores = jnp.einsum('...td,...sd->...ts', query_block.astype(jnp.float32), prev_keys.astype(jnp.float32)) * inverse_root
    query_pos = lax.broadcasted_iota(jnp.int32, (BLK, BLK), 0)
    key_pos = lax.broadcasted_iota(jnp.int32, (BLK, BLK), 1)
    pair_mask = usable[..., None, None] & (key_pos > query_pos + BLK - window_width[..., None, None])
    scores = temper[..., None, None] * raw_scores
    row_top = lax.optimization_barrier(jnp.max(jnp.where(pair_mask, scores, blocked_score), axis=-1))
    weights = jnp.where(pair_mask, jnp.exp(scores - row_top[..., None]), 0.0)
    prob_grad = jnp.einsum('...td,...sd->...ts', grad_block.astype(jnp.float32), prev_values.astype(jnp.float32))
    return (raw_scores, pair_mask, prob_grad, row_top, lax.optimization_barrier(jnp.sum(weights, axis=-1)), lax.optimization_barrier(jnp.sum(weights * prob_grad, axis=-1)))

def window_grads(raw_scores, pair_mask, prob_grad, query_block, prev_keys, grad_block, log_total, row_delta, temper):
    inverse_root = 1.0 / math.sqrt(HD)
    scaling = (temper * inverse_root)[..., None, None]
    probability = jnp.where(pair_mask, jnp.exp(temper[..., None, None] * raw_scores - log_total[..., None]), 0.0)
    score_grad = probability * (prob_grad - row_delta[..., None])
    prob_low = lifted(probability)
    grad_low = lifted(score_grad)
    query_part = jnp.einsum('...ts,...sd->...td', grad_low, prev_keys.astype(jnp.float32)) * scaling
    key_part = jnp.einsum('...ts,...td->...sd', grad_low, query_block.astype(jnp.float32)) * scaling
    value_part = jnp.einsum('...ts,...td->...sd', prob_low, grad_block.astype(jnp.float32))
    temper_part = lax.optimization_barrier(jnp.sum(score_grad * raw_scores, axis=(-2, -1)))
    return (query_part, key_part, value_part, temper_part)

def cluster_pair(query_items, key_items, value_items, grad_items, live_items, temper, window_top, window_total, window_mass):
    row_count = MOST * BLK
    inverse_root = 1.0 / math.sqrt(HD)
    scaling = temper * inverse_root
    query_rows = query_items.reshape(row_count, HD)
    key_rows = key_items.reshape(row_count, HD)
    value_rows = value_items.reshape(row_count, HD)
    grad_rows = grad_items.reshape(row_count, HD)
    item_of = jnp.arange(row_count) // BLK
    token_of = jnp.arange(row_count) % BLK
    live_rows = jnp.repeat(live_items, BLK)
    earlier = (item_of[None, :] < item_of[:, None]) | (item_of[None, :] == item_of[:, None]) & (token_of[None, :] <= token_of[:, None])
    pair_mask = live_rows[:, None] & live_rows[None, :] & earlier
    top_rows = window_top.reshape(row_count)
    total_rows = window_total.reshape(row_count)
    mass_rows = window_mass.reshape(row_count)
    raw_scores = jnp.dot(query_rows, key_rows.T, preferred_element_type=jnp.float32) * inverse_root
    scores = temper * raw_scores
    row_top = jnp.maximum(lax.optimization_barrier(jnp.max(jnp.where(pair_mask, scores, blocked_score), axis=1)), top_rows)
    weights = jnp.where(pair_mask, jnp.exp(scores - row_top[:, None]), 0.0)
    row_total = lax.optimization_barrier(jnp.sum(weights, axis=1)) + total_rows * jnp.exp(top_rows - row_top)
    log_total = row_top + jnp.log(jnp.where(live_rows, row_total, 1.0))
    probability = jnp.where(pair_mask, jnp.exp(scores - log_total[:, None]), 0.0)
    prob_grad = jnp.dot(grad_rows, value_rows.T, preferred_element_type=jnp.float32)
    row_delta = lax.optimization_barrier(jnp.sum(probability * prob_grad, axis=1)) + mass_rows * jnp.exp(top_rows - log_total)
    score_grad = probability * (prob_grad - row_delta[:, None])
    prob_low = probability.astype(jnp.bfloat16)
    grad_low = score_grad.astype(jnp.bfloat16)
    query_part = jnp.dot(grad_low, key_rows, preferred_element_type=jnp.float32) * scaling
    key_part = jnp.dot(grad_low.T, query_rows, preferred_element_type=jnp.float32) * scaling
    value_part = jnp.dot(prob_low.T, grad_rows, preferred_element_type=jnp.float32)
    temper_part = jnp.sum(score_grad * raw_scores)
    return (query_part.reshape(MOST, BLK, HD), log_total.reshape(MOST, BLK), row_delta.reshape(MOST, BLK), key_part.reshape(MOST, BLK, HD), value_part.reshape(MOST, BLK, HD), temper_part)

def reference(probe_vectors, lookup_vectors, content_vectors, result_cotangent, logit_softness, block_grouping, neighborhood_span):

    def heads_first(array_in):
        return array_in.reshape(CORPUS_SIZE, NBLK, BLK, ATTENTION_SPLITS, HD).transpose(0, 3, 1, 2, 4).reshape(CORPUS_SIZE * ATTENTION_SPLITS, NBLK, BLK, HD)
    split_probes = heads_first(probe_vectors)
    split_lookups = heads_first(lookup_vectors)
    split_contents = heads_first(content_vectors)
    split_derivatives = heads_first(result_cotangent)
    split_numbers = block_grouping[..., 0].reshape(CORPUS_SIZE * ATTENTION_SPLITS, NBLK).astype(jnp.int32)
    split_softness = jnp.tile(logit_softness, CORPUS_SIZE)
    split_dimension = jnp.tile(neighborhood_span, CORPUS_SIZE).astype(jnp.int32)

    def single_split(head_inputs):
        query_h, key_h, value_h, grad_h, ids_h, temper, width_h = head_inputs
        empty = jnp.zeros((1, BLK, HD), query_h.dtype)
        prev_keys = jnp.concatenate([empty, key_h[:-1]], axis=0)
        prev_values = jnp.concatenate([empty, value_h[:-1]], axis=0)
        before = jnp.concatenate([jnp.full((1,), -1, jnp.int32), ids_h[:-1]])
        usable = (jnp.arange(NBLK) >= 1) & (before != ids_h)
        raw_w, mask_w, pgrad_w, top_w, total_w, mass_w = window_parts(query_h, prev_keys, prev_values, grad_h, usable, width_h, temper)

        def one_cluster(cluster):
            member = ids_h == cluster
            member_rank = jnp.cumsum(member.astype(jnp.int32)) - 1
            member_count = jnp.sum(member.astype(jnp.int32))
            picked = member[None, :] & (member_rank[None, :] == jnp.arange(MOST)[:, None])
            member_block = lax.optimization_barrier(jnp.sum(jnp.where(picked, jnp.arange(NBLK)[None, :], 0), axis=1)).astype(jnp.int32)
            live_items = jnp.arange(MOST) < member_count
            results = cluster_pair(query_h[member_block], key_h[member_block], value_h[member_block], grad_h[member_block], live_items, temper, top_w[member_block], total_w[member_block], mass_w[member_block])
            return results + (member_block, live_items)
        query_c, log_c, delta_c, key_c, value_c, temper_c, member_block, live_items = lax.map(one_cluster, jnp.arange(NC, dtype=jnp.int32))
        flat_block = member_block.reshape(-1)
        flat_live = live_items.reshape(-1)

        def spread(part):
            shaped = part.reshape((NC * MOST,) + part.shape[2:])
            chosen = jnp.where(flat_live.reshape((-1,) + (1,) * (shaped.ndim - 1)), shaped, 0.0)
            return jnp.zeros((NBLK,) + part.shape[2:], part.dtype).at[flat_block].add(chosen)
        query_cl = spread(query_c)
        log_total = spread(log_c)
        row_delta = spread(delta_c)
        key_cl = spread(key_c)
        value_cl = spread(value_c)
        query_w, key_w, value_w, temper_w = window_grads(raw_w, mask_w, pgrad_w, query_h, prev_keys, grad_h, log_total, row_delta, temper)
        tail_zero = jnp.zeros((1, BLK, HD), jnp.float32)
        key_next = jnp.concatenate([key_w[1:], tail_zero], axis=0)
        value_next = jnp.concatenate([value_w[1:], tail_zero], axis=0)
        query_out = (lifted(query_cl) + lifted(query_w)).astype(jnp.bfloat16)
        key_out = (lifted(key_cl) + lifted(key_next)).astype(jnp.bfloat16)
        value_out = (lifted(value_cl) + lifted(value_next)).astype(jnp.bfloat16)
        return (query_out, key_out, value_out, jnp.sum(temper_c) + jnp.sum(temper_w))
    derivative_wrt_probe, derivative_wrt_lookup, derivative_wrt_content, softness_accumulations = lax.map(single_split, (split_probes, split_lookups, split_contents, split_derivatives, split_numbers, split_softness, split_dimension))

    def tokens_first(array_in):
        return array_in.reshape(CORPUS_SIZE, ATTENTION_SPLITS, NBLK, BLK, HD).transpose(0, 2, 3, 1, 4).reshape(CORPUS_SIZE, SEQLEN, ATTENTION_SPLITS * HD)
    temper_grad = lax.optimization_barrier(jnp.sum(softness_accumulations.reshape(CORPUS_SIZE, ATTENTION_SPLITS), axis=0)) / (CORPUS_SIZE * SEQLEN)
    return (tokens_first(derivative_wrt_probe), tokens_first(derivative_wrt_lookup), tokens_first(derivative_wrt_content), temper_grad)
```

```python
import functools
import math

import jax
import jax.numpy as jnp
from jax import lax
from jax.experimental import pallas as pl
from jax.experimental.pallas import tpu as pltpu
from jax.sharding import PartitionSpec as P

HD = 128
BLK = 128
MOST = 12
NC = 8
HEADS = 16
Z = 8
CHIPS = 32
BLOCKS = 64
DOCS = 4
OFF = -1e30
F32 = jnp.float32
BF16 = jnp.bfloat16


def chip_of(head):
    row = head // 4
    return row * Z + 2 * (head % 4) + row % 2


def place():
    me = lax.axis_index("seq")
    chip = me // 2
    row, col = chip // Z, chip % Z
    serves = (row + col) % 2 == 0
    return me, chip, me % 2, serves, row * 4 + col // 2


def loop(count, body):
    def step(i, carry):
        body(i)
        return carry

    lax.fori_loop(0, count, step, 0)


def head_cols(head):
    return pl.ds(pl.multiple_of(head * HD, HD), HD)


def scatter_kernel(q_ref, k_ref, v_ref, g_ref, qg_ref, kv_ref, send_sem, qg_sem, kv_sem, pass_send, pass_recv):
    me, chip, core, serves, _ = place()
    partner = me + 1 - 2 * core
    barrier = pltpu.get_barrier_semaphore()

    @pl.when(serves)
    def _():
        def greet(s):
            @pl.when(s != chip)
            def _():
                pl.semaphore_signal(barrier, inc=1, device_id={"seq": 2 * s + core})

        loop(CHIPS, greet)
        pl.semaphore_signal(barrier, inc=1, device_id={"seq": partner})

    pl.semaphore_wait(barrier, HEADS)

    def pieces(head):
        cols = head_cols(head)
        return (
            (k_ref.at[0, :, cols], kv_ref.at[me, 0], kv_sem.at[chip]),
            (v_ref.at[0, :, cols], kv_ref.at[me, 1], kv_sem.at[chip]),
            (q_ref.at[0, :, cols], qg_ref.at[chip, 0], qg_sem.at[chip]),
            (g_ref.at[0, :, cols], qg_ref.at[chip, 1], qg_sem.at[chip]),
        )

    def send(turn):
        head = (turn + chip // 2) % HEADS
        target = 2 * chip_of(head) + core

        @pl.when(target != me)
        def _():
            for src, dst, sem in pieces(head):
                pltpu.make_async_remote_copy(
                    src_ref=src,
                    dst_ref=dst,
                    send_sem=send_sem.at[head],
                    recv_sem=sem,
                    device_id={"seq": target},
                ).start()

        @pl.when(target == me)
        def _():
            for src, dst, sem in pieces(head):
                pltpu.make_async_copy(src, dst, sem).start()

    loop(HEADS, send)

    def handed(s):
        block = 2 * s + core
        return pltpu.make_async_remote_copy(
            src_ref=kv_ref.at[block],
            dst_ref=kv_ref.at[block],
            send_sem=pass_send.at[s],
            recv_sem=pass_recv.at[s],
            device_id={"seq": partner},
        )

    @pl.when(serves)
    def _():
        def take(turn):
            s = (turn + chip) % CHIPS
            block = 2 * s + core
            pltpu.make_async_copy(kv_ref.at[block], kv_ref.at[block], kv_sem.at[s]).wait()
            handed(s).start()

        loop(CHIPS, take)

        def finish(s):
            other = 2 * s + 1 - core
            pltpu.make_async_copy(qg_ref.at[s], qg_ref.at[s], qg_sem.at[s]).wait()
            pltpu.make_async_copy(kv_ref.at[other], kv_ref.at[other], pass_recv.at[s]).wait()
            handed(s).wait_send()

        loop(CHIPS, finish)

    def sent(head):
        @pl.when(2 * chip_of(head) + core != me)
        def _():
            whole = kv_ref.at[pl.ds(0, 2)]
            pltpu.make_async_copy(whole, whole, send_sem.at[head]).wait()

    loop(HEADS, sent)


def scatter_blocks(q, k, v, g):
    hbm = pl.BlockSpec(memory_space=pl.ANY)
    return pl.pallas_call(
        scatter_kernel,
        out_shape=(
            jax.ShapeDtypeStruct((CHIPS, 2, BLK, HD), BF16),
            jax.ShapeDtypeStruct((BLOCKS, 2, BLK, HD), BF16),
        ),
        in_specs=[hbm] * 4,
        out_specs=(hbm, hbm),
        scratch_shapes=[
            pltpu.SemaphoreType.DMA((HEADS,)),
            pltpu.SemaphoreType.DMA((CHIPS,)),
            pltpu.SemaphoreType.DMA((CHIPS,)),
            pltpu.SemaphoreType.DMA((CHIPS,)),
            pltpu.SemaphoreType.DMA((CHIPS,)),
        ],
        compiler_params=pltpu.CompilerParams(collective_id=1, has_side_effects=True),
        name="scatter_blocks",
    )(q, k, v, g)


def dot_nt(a, b):
    return lax.dot_general(a, b, (((1,), (1,)), ((), ())), preferred_element_type=F32)


def attend_kernel(
    where_ref,
    ids_ref,
    soft_ref,
    span_ref,
    qg_ref,
    kv_hbm,
    dq_ref,
    own_ref,
    oth_ref,
    temper_ref,
    k_sc,
    v_sc,
    kt_sc,
    dk_acc,
    dv_acc,
    s_sc,
    d_sc,
    p_sc,
    e_sc,
    t_acc,
    slot_ref,
    count_ref,
    sems,
):
    core, serves, head = where_ref[0], where_ref[1], where_ref[2]
    inverse_root = 1.0 / math.sqrt(HD)
    log2e = 1.4426950408889634

    @pl.when(serves == 1)
    def _():
        temper = soft_ref[head]
        width = span_ref[head]
        scale = temper * inverse_root
        power = scale * log2e

        def clear(c):
            count_ref[c] = 0

        loop(NC, clear)

        def fetch(b):
            cluster = ids_ref[head, b]
            rank = count_ref[cluster]
            count_ref[cluster] = rank + 1
            slot = cluster * MOST + rank
            slot_ref[b] = slot
            rows = pl.ds(pl.multiple_of(slot * BLK, BLK), BLK)
            pltpu.make_async_copy(kv_hbm.at[b, 0], k_sc.at[rows], sems.at[0]).start()
            pltpu.make_async_copy(kv_hbm.at[b, 1], v_sc.at[rows], sems.at[1]).start()

        loop(BLOCKS, fetch)
        t_acc[...] = jnp.zeros_like(t_acc)

        def zero(i):
            rows = pl.ds(pl.multiple_of(i * BLK, BLK), BLK)
            dk_acc[rows, :] = jnp.zeros((BLK, HD), F32)
            dv_acc[rows, :] = jnp.zeros((BLK, HD), F32)

        loop(NC * MOST, zero)
        eye = (
            lax.broadcasted_iota(jnp.int32, (HD, HD), 0)
            == lax.broadcasted_iota(jnp.int32, (HD, HD), 1)
        ).astype(BF16)
        gap = lax.broadcasted_iota(jnp.int32, (BLK, BLK), 0) - lax.broadcasted_iota(
            jnp.int32, (BLK, BLK), 1
        )
        all_rows = pl.ds(0, BLOCKS * BLK)
        pltpu.make_async_copy(k_sc.at[all_rows], k_sc.at[all_rows], sems.at[0]).wait()
        pltpu.make_async_copy(v_sc.at[all_rows], v_sc.at[all_rows], sems.at[1]).wait()

        def blank(c):
            @pl.when(count_ref[c] % 2 == 1)
            def _():
                rows = pl.ds(pl.multiple_of((c * MOST + count_ref[c]) * BLK, BLK), BLK)
                k_sc[rows, :] = jnp.zeros((BLK, HD), BF16)
                v_sc[rows, :] = jnp.zeros((BLK, HD), BF16)
                kt_sc[:, rows] = jnp.zeros((HD, BLK), BF16)

        loop(NC, blank)

        def turn_keys(b):
            start = pl.multiple_of(slot_ref[b] * BLK, BLK)
            kt_sc[:, pl.ds(start, BLK)] = dot_nt(eye, k_sc[pl.ds(start, BLK), :]).astype(BF16)

        loop(BLOCKS, turn_keys)

        def query_block(i, block, slot, cluster, rank, blocks):
            rows = blocks * BLK
            q = qg_ref[i, 0]
            g = qg_ref[i, 1]
            first = pl.multiple_of(cluster * (MOST * BLK), BLK)
            span = pl.ds(first, rows)
            before = jnp.maximum(block - 1, 0)
            before_slot = slot_ref[before]
            usable = (block >= 1) & (before_slot // MOST != cluster)
            edge = jnp.where(usable, BLK - width, 2 * BLK)
            wstart = pl.multiple_of(before_slot * BLK, BLK)
            wspan = pl.ds(wstart, BLK)
            limit = (rank - blocks + 2) * BLK

            s_sc[pl.ds(0, rows), :] = dot_nt(k_sc[span, :], q)
            d_sc[pl.ds(0, rows), :] = dot_nt(v_sc[span, :], g)
            s_win = jnp.where(gap > edge, dot_nt(k_sc[wspan, :], q), OFF)
            s_sc[pl.ds(rows, BLK), :] = s_win
            d_sc[pl.ds(rows, BLK), :] = dot_nt(v_sc[wspan, :], g)
            for j in (blocks - 2, blocks - 1):
                part = pl.ds(j * BLK, BLK)
                shift = (j - blocks + 2) * BLK
                s_sc[part, :] = jnp.where(gap <= limit - shift, s_sc[part, :], OFF)
            top = jnp.full((8, BLK), OFF, F32)
            for j in range(blocks + 1):
                tile = s_sc[pl.ds(j * BLK, BLK), :]
                top = jnp.maximum(top, jnp.max(tile.reshape(BLK // 8, 8, BLK), axis=0))
            top = jnp.max(top, axis=0, keepdims=True)
            total = jnp.zeros((8, BLK), F32)
            mass = jnp.zeros((8, BLK), F32)
            for j in range(blocks + 1):
                part = pl.ds(j * BLK, BLK)
                weight = jnp.exp2((s_sc[part, :] - top) * power)
                p_sc[part, :] = weight
                total = total + jnp.sum(weight.reshape(BLK // 8, 8, BLK), axis=0)
                mass = mass + jnp.sum((weight * d_sc[part, :]).reshape(BLK // 8, 8, BLK), axis=0)
            inverse = 1.0 / jnp.sum(total, axis=0, keepdims=True)
            delta = jnp.sum(mass, axis=0, keepdims=True) * inverse
            terms = jnp.zeros((8, BLK), F32)
            for j in range(blocks + 1):
                part = pl.ds(j * BLK, BLK)
                prob = p_sc[part, :] * inverse
                score = prob * (d_sc[part, :] - delta)
                terms = terms + jnp.sum((score * s_sc[part, :]).reshape(BLK // 8, 8, BLK), axis=0)
                e_sc[0, part, :] = prob.astype(BF16)
                e_sc[1, part, :] = score.astype(BF16)
            t_acc[...] += terms
            body = pl.ds(0, rows)
            tail = pl.ds(rows, BLK)
            dv_acc[span, :] += jnp.dot(e_sc[0, body, :], g, preferred_element_type=F32)
            dv_acc[wspan, :] += jnp.dot(e_sc[0, tail, :], g, preferred_element_type=F32)
            dk_acc[span, :] += jnp.dot(e_sc[1, body, :], q, preferred_element_type=F32)
            dk_acc[wspan, :] += jnp.dot(e_sc[1, tail, :], q, preferred_element_type=F32)
            turned = jnp.dot(kt_sc[:, span], e_sc[1, body, :], preferred_element_type=F32)
            turned += jnp.dot(kt_sc[:, wspan], e_sc[1, tail, :], preferred_element_type=F32)
            dq_ref[i] = (turned * scale).T.astype(BF16)

        def query_step(i):
            block = 2 * i + core
            slot = slot_ref[block]
            cluster = slot // MOST
            rank = slot % MOST
            for blocks in range(2, MOST + 1, 2):

                @pl.when(rank // 2 == blocks // 2 - 1)
                def _():
                    query_block(i, block, slot, cluster, rank, blocks)

        loop(CHIPS, query_step)

        def give(i):
            mine = pl.ds(pl.multiple_of(slot_ref[2 * i + core] * BLK, BLK), BLK)
            other = pl.ds(pl.multiple_of(slot_ref[2 * i + 1 - core] * BLK, BLK), BLK)
            own_ref[i, 0] = dk_acc[mine, :] * scale
            own_ref[i, 1] = dv_acc[mine, :]
            oth_ref[i, 0] = (dk_acc[other, :] * scale).astype(BF16)
            oth_ref[i, 1] = dv_acc[other, :].astype(BF16)

        loop(CHIPS, give)
        whole = jnp.sum(jnp.sum(t_acc[...], axis=0, keepdims=True), axis=1, keepdims=True)
        temper_ref[0] = jnp.broadcast_to(whole * inverse_root, (1, BLK))


def attend(where, ids, soft, span, qg, kv):
    smem = pl.BlockSpec(memory_space=pltpu.SMEM)
    vmem = pl.BlockSpec(memory_space=pltpu.VMEM)
    slots = NC * MOST * BLK
    return pl.pallas_call(
        attend_kernel,
        out_shape=(
            jax.ShapeDtypeStruct((CHIPS, BLK, HD), BF16),
            jax.ShapeDtypeStruct((CHIPS, 2, BLK, HD), F32),
            jax.ShapeDtypeStruct((CHIPS, 2, BLK, HD), BF16),
            jax.ShapeDtypeStruct((1, 1, BLK), F32),
        ),
        in_specs=[smem, smem, smem, smem, vmem, pl.BlockSpec(memory_space=pl.ANY)],
        out_specs=(vmem, vmem, vmem, vmem),
        scratch_shapes=[
            pltpu.VMEM((slots, HD), BF16),
            pltpu.VMEM((slots, HD), BF16),
            pltpu.VMEM((HD, slots), BF16),
            pltpu.VMEM((slots, HD), F32),
            pltpu.VMEM((slots, HD), F32),
            pltpu.VMEM(((MOST + 1) * BLK, BLK), F32),
            pltpu.VMEM(((MOST + 1) * BLK, BLK), F32),
            pltpu.VMEM(((MOST + 1) * BLK, BLK), F32),
            pltpu.VMEM((2, (MOST + 1) * BLK, BLK), BF16),
            pltpu.VMEM((8, BLK), F32),
            pltpu.SMEM((BLOCKS,), jnp.int32),
            pltpu.SMEM((NC,), jnp.int32),
            pltpu.SemaphoreType.DMA((2,)),
        ],
        name="attend",
    )(where, ids, soft, span, qg, kv)


CHUNKS = 8
PER = CHIPS // CHUNKS
PEERS = DOCS * 2


def gather_kernel(
    dq_in,
    own_in,
    oth_in,
    temper_in,
    dq_ref,
    dk_ref,
    dv_ref,
    temper_ref,
    own_v,
    their_v,
    res_v,
    t_heads,
    t_all,
    own_sem,
    their_send,
    their_recv,
    home_send,
    home_recv,
    temper_send,
    temper_recv,
    peer_send,
    peer_recv,
):
    me, chip, core, serves, head = place()
    doc = lax.axis_index("dp")
    partner = me + 1 - 2 * core
    my_peer = doc * 2 + core
    barrier = pltpu.get_barrier_semaphore()

    def peer_id(j):
        return {"seq": 2 * chip + j % 2, "dp": j // 2}

    def greet_server(h):
        target = 2 * chip_of(h) + core

        @pl.when(target != me)
        def _():
            pl.semaphore_signal(barrier, inc=1, device_id={"seq": target})

    loop(HEADS, greet_server)

    def greet_peer(j):
        @pl.when(j != my_peer)
        def _():
            pl.semaphore_signal(barrier, inc=1, device_id=peer_id(j))

    loop(PEERS, greet_peer)
    pl.semaphore_wait(barrier, jnp.where(serves, CHIPS - 1 + PEERS - 1, PEERS - 1))

    def home(s, src, dst, lane, start):
        target = 2 * s + core

        @pl.when(target != me)
        def _():
            copy = pltpu.make_async_remote_copy(
                src_ref=src,
                dst_ref=dst,
                send_sem=home_send.at[lane, s],
                recv_sem=home_recv.at[lane, head],
                device_id={"seq": target},
            )
            if start:
                copy.start()
            else:
                copy.wait_send()

        if start:

            @pl.when(target == me)
            def _():
                pltpu.make_async_copy(src, dst, home_recv.at[lane, head]).start()

    def home_dq(s, start):
        home(s, dq_in.at[s], dq_ref.at[0, :, head_cols(head)], 0, start)

    def home_dk(s, start):
        home(s, res_v.at[s, 0], dk_ref.at[0, :, head_cols(head)], 1, start)

    def home_dv(s, start):
        home(s, res_v.at[s, 1], dv_ref.at[0, :, head_cols(head)], 2, start)

    def home_temper(s, start):
        target = 2 * s + core

        @pl.when(target != me)
        def _():
            copy = pltpu.make_async_remote_copy(
                src_ref=temper_in.at[0],
                dst_ref=t_heads.at[head],
                send_sem=temper_send.at[s],
                recv_sem=temper_recv.at[head],
                device_id={"seq": target},
            )
            if start:
                copy.start()
            else:
                copy.wait_send()

        if start:

            @pl.when(target == me)
            def _():
                pltpu.make_async_copy(temper_in.at[0], t_heads.at[head], temper_recv.at[head]).start()

    def theirs(j):
        part = pl.ds(j * PER, PER)
        return pltpu.make_async_remote_copy(
            src_ref=oth_in.at[part],
            dst_ref=their_v.at[part],
            send_sem=their_send.at[j],
            recv_sem=their_recv.at[j],
            device_id={"seq": partner},
        )

    def mine(j):
        part = pl.ds(j * PER, PER)
        return pltpu.make_async_copy(own_in.at[part], own_v.at[part], own_sem.at[j])

    def turned(i):
        return (i + chip) % CHIPS

    @pl.when(serves)
    def _():
        def begin(j):
            theirs(j).start()
            mine(j).start()

        loop(CHUNKS, begin)

        def send_first(i):
            s = turned(i)
            home_temper(s, True)
            home_dq(s, True)

        loop(CHIPS, send_first)

        def add(j):
            mine(j).wait()
            theirs(j).wait_recv()

            def add_one(i):
                s = j * PER + i
                res_v[s, 0] = (own_v[s, 0] + their_v[s, 0].astype(F32)).astype(BF16)
                res_v[s, 1] = (own_v[s, 1] + their_v[s, 1].astype(F32)).astype(BF16)

            loop(PER, add_one)

        loop(CHUNKS, add)

        def send_rest(i):
            s = turned(i)
            home_dk(s, True)
            home_dv(s, True)

        loop(CHIPS, send_rest)

    def heard(h):
        pltpu.make_async_copy(t_heads.at[h], t_heads.at[h], temper_recv.at[h]).wait()

    loop(HEADS, heard)

    def tell(j):
        return pltpu.make_async_remote_copy(
            src_ref=t_heads,
            dst_ref=t_all.at[my_peer],
            send_sem=peer_send.at[j],
            recv_sem=peer_recv.at[my_peer],
            device_id=peer_id(j),
        )

    def tell_peer(j):
        @pl.when(j != my_peer)
        def _():
            tell(j).start()

        @pl.when(j == my_peer)
        def _():
            pltpu.make_async_copy(t_heads, t_all.at[my_peer], peer_recv.at[my_peer]).start()

    loop(PEERS, tell_peer)

    def landed(h):
        cols = head_cols(h)
        for lane, ref in enumerate((dq_ref, dk_ref, dv_ref)):
            piece = ref.at[0, :, cols]
            pltpu.make_async_copy(piece, piece, home_recv.at[lane, h]).wait()

    loop(HEADS, landed)

    def told(j):
        pltpu.make_async_copy(t_all.at[j], t_all.at[j], peer_recv.at[j]).wait()

    loop(PEERS, told)
    total = t_all[0]
    for j in range(1, PEERS):
        total = total + t_all[j]
    temper_ref[...] = total

    def spoken(j):
        @pl.when(j != my_peer)
        def _():
            tell(j).wait_send()

    loop(PEERS, spoken)

    @pl.when(serves)
    def _():
        def close(j):
            theirs(j).wait_send()

        loop(CHUNKS, close)

        def sent(s):
            home_temper(s, False)
            home_dq(s, False)
            home_dk(s, False)
            home_dv(s, False)

        loop(CHIPS, sent)


def gather_grads(dq, own, oth, temper):
    hbm = pl.BlockSpec(memory_space=pl.ANY)
    vmem = pl.BlockSpec(memory_space=pltpu.VMEM)
    whole = jax.ShapeDtypeStruct((1, BLK, HEADS * HD), BF16)
    dma = pltpu.SemaphoreType.DMA
    return pl.pallas_call(
        gather_kernel,
        out_shape=(whole, whole, whole, jax.ShapeDtypeStruct((HEADS, 1, BLK), F32)),
        in_specs=[hbm, hbm, hbm, vmem],
        out_specs=(hbm, hbm, hbm, vmem),
        scratch_shapes=[
            pltpu.VMEM((CHIPS, 2, BLK, HD), F32),
            pltpu.VMEM((CHIPS, 2, BLK, HD), BF16),
            pltpu.VMEM((CHIPS, 2, BLK, HD), BF16),
            pltpu.VMEM((HEADS, 1, BLK), F32),
            pltpu.VMEM((PEERS, HEADS, 1, BLK), F32),
            dma((CHUNKS,)),
            dma((CHUNKS,)),
            dma((CHUNKS,)),
            dma((3, CHIPS)),
            dma((3, HEADS)),
            dma((CHIPS,)),
            dma((HEADS,)),
            dma((PEERS,)),
            dma((PEERS,)),
        ],
        compiler_params=pltpu.CompilerParams(collective_id=2, has_side_effects=True),
        name="gather_grads",
    )(dq, own, oth, temper)


def shards(q, k, v, g, softness, grouping, span):
    _, _, core, serves, head = place()
    qg, kv = scatter_blocks(q, k, v, g)
    where = jnp.stack([core, serves.astype(jnp.int32), head])
    dq, own, oth, temper = attend(where, grouping.reshape(HEADS, BLOCKS), softness, span, qg, kv)
    dq, dk, dv, temper = gather_grads(dq, own, oth, temper)
    return dq, dk, dv, temper[:, 0, 0] / (DOCS * BLOCKS * BLK)


def solution(mesh):
    tokens = P("dp", "seq", None)
    return jax.shard_map(
        shards,
        mesh=mesh,
        in_specs=(tokens, tokens, tokens, tokens, P(), P("dp", None, None, None), P()),
        out_specs=(tokens, tokens, tokens, P()),
        check_vma=False,
    )
```

```python
import math

import jax
import jax.numpy as jnp
from jax import lax
from jax.experimental import pallas as pl
from jax.experimental.pallas import tpu as pltpu
from jax.sharding import PartitionSpec as P

HD = 128
BLK = 128
MOST = 12
NC = 8
HEADS = 16
Z = 8
CHIPS = 32
BLOCKS = 64
DOCS = 4
OFF = -1e30
F32 = jnp.float32
BF16 = jnp.bfloat16


def place():
    me = lax.axis_index("seq")
    row, col = me // (2 * Z), (me // 2) % Z
    core = me % 2
    inner = ((row + 1) // 2) % 2
    partner = me + 1 - 2 * core
    neighbour = me + 2 * Z * (1 - 2 * (row % 2))
    return me, row, col, core, inner, (row // 2) * Z + col, partner, neighbour


def row_of(half, inner):
    return half * (3 - 2 * inner) + inner


def member(i, inner, core):
    return 2 * (row_of(i // Z, inner) * Z + i % Z) + core


def loop(count, body):
    def step(i, carry):
        body(i)
        return carry

    lax.fori_loop(0, count, step, 0)


def head_cols(head):
    return pl.ds(pl.multiple_of(head * HD, HD), HD)


def in_turn(turn, col, way):
    k = turn // 2
    distance = jnp.where(k % 2 == 1, 4 - (k + 1) // 2, 4 + k // 2)
    return (turn % 2) * Z + (col + way * distance + Z) % Z


def scatter_kernel(
    q_ref, k_ref, v_ref, g_ref, qg_ref, kv_ref, send_sem, qg_sem, kv_sem, near_send, near_recv, pass_send, pass_recv
):
    me, _, col, core, inner, head, partner, neighbour = place()
    barrier = pltpu.get_barrier_semaphore()

    def greet(i):
        @pl.when(i != head)
        def _():
            pl.semaphore_signal(barrier, inc=1, device_id={"seq": member(i, inner, core)})

    loop(HEADS, greet)
    pl.semaphore_signal(barrier, inc=1, device_id={"seq": partner})
    pl.semaphore_signal(barrier, inc=1, device_id={"seq": neighbour})
    pl.semaphore_wait(barrier, HEADS + 1)

    def pieces(h):
        cols = head_cols(h)
        return (
            (k_ref.at[0, :, cols], kv_ref.at[me, 0], kv_sem.at[head]),
            (v_ref.at[0, :, cols], kv_ref.at[me, 1], kv_sem.at[head]),
            (q_ref.at[0, :, cols], qg_ref.at[head, 0], qg_sem.at[head]),
            (g_ref.at[0, :, cols], qg_ref.at[head, 1], qg_sem.at[head]),
        )

    for src, dst, sem in pieces(head):
        pltpu.make_async_copy(src, dst, sem).start()

    def send(turn):
        h = in_turn(turn, col, 1)

        @pl.when(h != head)
        def _():
            for src, dst, sem in pieces(h):
                pltpu.make_async_remote_copy(
                    src_ref=src,
                    dst_ref=dst,
                    send_sem=send_sem.at[h],
                    recv_sem=sem,
                    device_id={"seq": member(h, inner, core)},
                ).start()

    loop(HEADS, send)

    def handed(block, target, send, recv):
        return pltpu.make_async_remote_copy(
            src_ref=kv_ref.at[block],
            dst_ref=kv_ref.at[block],
            send_sem=send,
            recv_sem=recv,
            device_id={"seq": target},
        )

    def to_near(s):
        return handed(member(s, inner, core), neighbour, near_send.at[s], near_recv.at[s])

    def to_partner(s):
        return handed(member(s, inner, core), partner, pass_send.at[s], pass_recv.at[s])

    def near_to_partner(s):
        return handed(member(s, 1 - inner, core), partner, pass_send.at[HEADS + s], pass_recv.at[HEADS + s])

    def arrived(block, sem):
        pltpu.make_async_copy(kv_ref.at[block], kv_ref.at[block], sem).wait()

    lag = 2

    def take(turn):
        @pl.when(turn < HEADS)
        def _():
            s = in_turn(turn, col, -1)
            arrived(member(s, inner, core), kv_sem.at[s])
            to_near(s).start()
            to_partner(s).start()

        @pl.when(turn >= lag)
        def _():
            s = in_turn(turn - lag, col, -1)
            arrived(member(s, 1 - inner, core), near_recv.at[s])
            near_to_partner(s).start()

    loop(HEADS + lag, take)

    def finish(s):
        pltpu.make_async_copy(qg_ref.at[s], qg_ref.at[s], qg_sem.at[s]).wait()
        arrived(member(s, inner, 1 - core), pass_recv.at[s])
        arrived(member(s, 1 - inner, 1 - core), pass_recv.at[HEADS + s])
        to_near(s).wait_send()
        to_partner(s).wait_send()
        near_to_partner(s).wait_send()

        @pl.when(s != head)
        def _():
            whole = kv_ref.at[pl.ds(0, 2)]
            pltpu.make_async_copy(whole, whole, send_sem.at[s]).wait()

    loop(HEADS, finish)


def scatter_blocks(q, k, v, g):
    hbm = pl.BlockSpec(memory_space=pl.ANY)
    return pl.pallas_call(
        scatter_kernel,
        out_shape=(
            jax.ShapeDtypeStruct((HEADS, 2, BLK, HD), BF16),
            jax.ShapeDtypeStruct((BLOCKS, 2, BLK, HD), BF16),
        ),
        in_specs=[hbm] * 4,
        out_specs=(hbm, hbm),
        scratch_shapes=[pltpu.SemaphoreType.DMA((HEADS,))] * 5
        + [pltpu.SemaphoreType.DMA((2 * HEADS,))] * 2,
        compiler_params=pltpu.CompilerParams(collective_id=1, has_side_effects=True),
        name="scatter_blocks",
    )(q, k, v, g)


def dot_nt(a, b):
    return lax.dot_general(a, b, (((1,), (1,)), ((), ())), preferred_element_type=F32)


def attend_kernel(
    ids_ref,
    soft_ref,
    span_ref,
    qg_ref,
    kv_hbm,
    dq_ref,
    own_ref,
    oth_ref,
    temper_ref,
    k_sc,
    v_sc,
    kt_sc,
    dk_acc,
    dv_acc,
    s_sc,
    d_sc,
    p_sc,
    e_sc,
    t_acc,
    slot_ref,
    count_ref,
    sems,
):
    _, _, _, core, inner, head, _, _ = place()
    inverse_root = 1.0 / math.sqrt(HD)
    log2e = 1.4426950408889634
    temper = soft_ref[head]
    width = span_ref[head]
    scale = temper * inverse_root
    power = scale * log2e

    def clear(c):
        count_ref[c] = 0

    loop(NC, clear)

    def fetch(b):
        cluster = ids_ref[head, b]
        rank = count_ref[cluster]
        count_ref[cluster] = rank + 1
        slot = cluster * MOST + rank
        slot_ref[b] = slot
        rows = pl.ds(pl.multiple_of(slot * BLK, BLK), BLK)
        pltpu.make_async_copy(kv_hbm.at[b, 0], k_sc.at[rows], sems.at[0]).start()
        pltpu.make_async_copy(kv_hbm.at[b, 1], v_sc.at[rows], sems.at[1]).start()

    loop(BLOCKS, fetch)
    t_acc[...] = jnp.zeros_like(t_acc)

    def zero(i):
        rows = pl.ds(pl.multiple_of(i * BLK, BLK), BLK)
        dk_acc[rows, :] = jnp.zeros((BLK, HD), F32)
        dv_acc[rows, :] = jnp.zeros((BLK, HD), F32)

    loop(NC * MOST, zero)
    eye = (
        lax.broadcasted_iota(jnp.int32, (HD, HD), 0)
        == lax.broadcasted_iota(jnp.int32, (HD, HD), 1)
    ).astype(BF16)
    gap = lax.broadcasted_iota(jnp.int32, (BLK, BLK), 0) - lax.broadcasted_iota(
        jnp.int32, (BLK, BLK), 1
    )
    all_rows = pl.ds(0, BLOCKS * BLK)
    pltpu.make_async_copy(k_sc.at[all_rows], k_sc.at[all_rows], sems.at[0]).wait()
    pltpu.make_async_copy(v_sc.at[all_rows], v_sc.at[all_rows], sems.at[1]).wait()

    def blank(c):
        @pl.when(count_ref[c] % 2 == 1)
        def _():
            rows = pl.ds(pl.multiple_of((c * MOST + count_ref[c]) * BLK, BLK), BLK)
            k_sc[rows, :] = jnp.zeros((BLK, HD), BF16)
            v_sc[rows, :] = jnp.zeros((BLK, HD), BF16)
            kt_sc[:, rows] = jnp.zeros((HD, BLK), BF16)

    loop(NC, blank)

    def turn_keys(group):
        for j in range(8):
            start = pl.multiple_of(slot_ref[group * 8 + j] * BLK, BLK)
            kt_sc[:, pl.ds(start, BLK)] = dot_nt(eye, k_sc[pl.ds(start, BLK), :]).astype(BF16)

    loop(BLOCKS // 8, turn_keys)

    def query_block(i, block, slot, cluster, rank, blocks):
        rows = blocks * BLK
        q = qg_ref[i, 0]
        g = qg_ref[i, 1]
        first = pl.multiple_of(cluster * (MOST * BLK), BLK)
        span = pl.ds(first, rows)
        before = jnp.maximum(block - 1, 0)
        before_slot = slot_ref[before]
        usable = (block >= 1) & (before_slot // MOST != cluster)
        edge = jnp.where(usable, BLK - width, 2 * BLK)
        wstart = pl.multiple_of(before_slot * BLK, BLK)
        wspan = pl.ds(wstart, BLK)
        limit = (rank - blocks + 2) * BLK

        s_sc[pl.ds(0, rows), :] = dot_nt(k_sc[span, :], q)
        d_sc[pl.ds(0, rows), :] = dot_nt(v_sc[span, :], g)
        s_win = jnp.where(gap > edge, dot_nt(k_sc[wspan, :], q), OFF)
        s_sc[pl.ds(rows, BLK), :] = s_win
        d_sc[pl.ds(rows, BLK), :] = dot_nt(v_sc[wspan, :], g)
        for j in (blocks - 2, blocks - 1):
            part = pl.ds(j * BLK, BLK)
            shift = (j - blocks + 2) * BLK
            s_sc[part, :] = jnp.where(gap <= limit - shift, s_sc[part, :], OFF)
        top = jnp.full((8, BLK), OFF, F32)
        for j in range(blocks + 1):
            tile = s_sc[pl.ds(j * BLK, BLK), :]
            top = jnp.maximum(top, jnp.max(tile.reshape(BLK // 8, 8, BLK), axis=0))
        top = jnp.max(top, axis=0, keepdims=True)
        total = jnp.zeros((8, BLK), F32)
        mass = jnp.zeros((8, BLK), F32)
        for j in range(blocks + 1):
            part = pl.ds(j * BLK, BLK)
            weight = jnp.exp2((s_sc[part, :] - top) * power)
            p_sc[part, :] = weight
            total = total + jnp.sum(weight.reshape(BLK // 8, 8, BLK), axis=0)
            mass = mass + jnp.sum((weight * d_sc[part, :]).reshape(BLK // 8, 8, BLK), axis=0)
        inverse = 1.0 / jnp.sum(total, axis=0, keepdims=True)
        delta = jnp.sum(mass, axis=0, keepdims=True) * inverse
        terms = jnp.zeros((8, BLK), F32)
        for j in range(blocks + 1):
            part = pl.ds(j * BLK, BLK)
            prob = p_sc[part, :] * inverse
            score = prob * (d_sc[part, :] - delta)
            terms = terms + jnp.sum((score * s_sc[part, :]).reshape(BLK // 8, 8, BLK), axis=0)
            e_sc[0, part, :] = prob.astype(BF16)
            e_sc[1, part, :] = score.astype(BF16)
        t_acc[...] += terms
        body = pl.ds(0, rows)
        tail = pl.ds(rows, BLK)
        dv_acc[span, :] += jnp.dot(e_sc[0, body, :], g, preferred_element_type=F32)
        dv_acc[wspan, :] += jnp.dot(e_sc[0, tail, :], g, preferred_element_type=F32)
        dk_acc[span, :] += jnp.dot(e_sc[1, body, :], q, preferred_element_type=F32)
        dk_acc[wspan, :] += jnp.dot(e_sc[1, tail, :], q, preferred_element_type=F32)
        turned = jnp.dot(kt_sc[:, span], e_sc[1, body, :], preferred_element_type=F32)
        turned += jnp.dot(kt_sc[:, wspan], e_sc[1, tail, :], preferred_element_type=F32)
        dq_ref[i] = (turned * scale).T.astype(BF16)

    def query_step(i):
        block = member(i, inner, core)
        slot = slot_ref[block]
        cluster = slot // MOST
        rank = slot % MOST
        for blocks in range(2, MOST + 1, 2):

            @pl.when(rank // 2 == blocks // 2 - 1)
            def _():
                query_block(i, block, slot, cluster, rank, blocks)

    loop(HEADS, query_step)

    def give(i):
        mine = pl.ds(pl.multiple_of(slot_ref[2 * i + core] * BLK, BLK), BLK)
        other = pl.ds(pl.multiple_of(slot_ref[2 * i + 1 - core] * BLK, BLK), BLK)
        own_ref[i, 0] = dk_acc[mine, :] * scale
        own_ref[i, 1] = dv_acc[mine, :]
        oth_ref[i, 0] = (dk_acc[other, :] * scale).astype(BF16)
        oth_ref[i, 1] = dv_acc[other, :].astype(BF16)

    loop(CHIPS, give)
    whole = jnp.sum(jnp.sum(t_acc[...], axis=0, keepdims=True), axis=1, keepdims=True)
    temper_ref[0] = jnp.broadcast_to(whole * inverse_root, (1, BLK))


def attend(ids, soft, span, qg, kv):
    smem = pl.BlockSpec(memory_space=pltpu.SMEM)
    vmem = pl.BlockSpec(memory_space=pltpu.VMEM)
    slots = NC * MOST * BLK
    return pl.pallas_call(
        attend_kernel,
        out_shape=(
            jax.ShapeDtypeStruct((HEADS, BLK, HD), BF16),
            jax.ShapeDtypeStruct((CHIPS, 2, BLK, HD), F32),
            jax.ShapeDtypeStruct((CHIPS, 2, BLK, HD), BF16),
            jax.ShapeDtypeStruct((1, 1, BLK), F32),
        ),
        in_specs=[smem, smem, smem, vmem, pl.BlockSpec(memory_space=pl.ANY)],
        out_specs=(vmem, vmem, vmem, vmem),
        scratch_shapes=[
            pltpu.VMEM((slots, HD), BF16),
            pltpu.VMEM((slots, HD), BF16),
            pltpu.VMEM((HD, slots), BF16),
            pltpu.VMEM((slots, HD), F32),
            pltpu.VMEM((slots, HD), F32),
            pltpu.VMEM(((MOST + 1) * BLK, BLK), F32),
            pltpu.VMEM(((MOST + 1) * BLK, BLK), F32),
            pltpu.VMEM(((MOST + 1) * BLK, BLK), F32),
            pltpu.VMEM((2, (MOST + 1) * BLK, BLK), BF16),
            pltpu.VMEM((8, BLK), F32),
            pltpu.SMEM((BLOCKS,), jnp.int32),
            pltpu.SMEM((NC,), jnp.int32),
            pltpu.SemaphoreType.DMA((2,)),
        ],
        name="attend",
    )(ids, soft, span, qg, kv)


CHUNKS = 8
PER = CHIPS // CHUNKS
HALF = CHUNKS // 2
PEERS = DOCS * 4


def chunk_of(u, inner):
    return 2 * row_of(u // 2, inner) + u % 2


def gather_kernel(
    dq_in,
    own_in,
    oth_in,
    temper_in,
    dq_ref,
    dk_ref,
    dv_ref,
    temper_ref,
    own_v,
    their_v,
    give_v,
    near_v,
    res_v,
    t_heads,
    t_all,
    own_sem,
    their_send,
    their_recv,
    near_send,
    near_recv,
    home_send,
    home_recv,
    temper_send,
    temper_recv,
    peer_send,
    peer_recv,
):
    me, row, col, core, inner, head, partner, neighbour = place()
    doc = lax.axis_index("dp")
    my_peer = doc * 4 + inner * 2 + core
    barrier = pltpu.get_barrier_semaphore()

    def peer_id(j):
        half = row // 2
        other = 2 * half + ((j // 2) % 2 + half) % 2
        return {"seq": 2 * (other * Z + col) + j % 2, "dp": j // 4}

    def greet_member(i):
        @pl.when(i != head)
        def _():
            pl.semaphore_signal(barrier, inc=1, device_id={"seq": member(i, inner, core)})

    loop(HEADS, greet_member)

    def greet_peer(j):
        @pl.when(j != my_peer)
        def _():
            pl.semaphore_signal(barrier, inc=1, device_id=peer_id(j))

    loop(PEERS, greet_peer)
    pl.semaphore_wait(barrier, HEADS - 1 + PEERS - 1)

    def home_copy(i, src, dst, lane):
        return pltpu.make_async_remote_copy(
            src_ref=src,
            dst_ref=dst.at[0, :, head_cols(head)],
            send_sem=home_send.at[lane, i],
            recv_sem=home_recv.at[lane, head],
            device_id={"seq": member(i, inner, core)},
        )

    def lanes(i):
        return (
            (dq_in.at[i], dq_ref, 0),
            (res_v.at[i, 0], dk_ref, 1),
            (res_v.at[i, 1], dv_ref, 2),
        )

    def go_home(i, src, dst, lane):
        @pl.when(i != head)
        def _():
            home_copy(i, src, dst, lane).start()

        @pl.when(i == head)
        def _():
            pltpu.make_async_copy(src, dst.at[0, :, head_cols(head)], home_recv.at[lane, head]).start()

    def temper_copy(i):
        return pltpu.make_async_remote_copy(
            src_ref=temper_in.at[0],
            dst_ref=t_heads.at[head],
            send_sem=temper_send.at[i],
            recv_sem=temper_recv.at[head],
            device_id={"seq": member(i, inner, core)},
        )

    def theirs(j):
        part = pl.ds(j * PER, PER)
        return pltpu.make_async_remote_copy(
            src_ref=oth_in.at[part],
            dst_ref=their_v.at[part],
            send_sem=their_send.at[j],
            recv_sem=their_recv.at[j],
            device_id={"seq": partner},
        )

    def mine(j):
        part = pl.ds(j * PER, PER)
        return pltpu.make_async_copy(own_in.at[part], own_v.at[part], own_sem.at[j])

    def near(u):
        part = pl.ds(u * PER, PER)
        return pltpu.make_async_remote_copy(
            src_ref=give_v.at[part],
            dst_ref=near_v.at[part],
            send_sem=near_send.at[u],
            recv_sem=near_recv.at[u],
            device_id={"seq": neighbour},
        )

    def chunk_in_order(step):
        return jnp.where(step < HALF, chunk_of(step % HALF, 1 - inner), chunk_of(step % HALF, inner))

    def begin(step):
        j = chunk_in_order(step)
        theirs(j).start()
        mine(j).start()

    loop(CHUNKS, begin)
    pltpu.make_async_copy(temper_in.at[0], t_heads.at[head], temper_recv.at[head]).start()

    def send_first(turn):
        i = in_turn(turn, col, 1)

        @pl.when(i != head)
        def _():
            temper_copy(i).start()

        go_home(i, *lanes(i)[0])

    loop(HEADS, send_first)

    def give(u):
        @pl.when(u < HALF)
        def _():
            j = chunk_of(u, 1 - inner)
            mine(j).wait()
            theirs(j).wait_recv()

            def add_one(i):
                for x in (0, 1):
                    total = own_v[j * PER + i, x] + their_v[j * PER + i, x].astype(F32)
                    give_v[u * PER + i, x] = total.astype(BF16)

            loop(PER, add_one)

        @pl.when(u > 0)
        def _():
            near(u - 1).start()

    loop(HALF + 1, give)

    def keep(u):
        @pl.when(u < HALF)
        def _():
            j = chunk_of(u, inner)
            mine(j).wait()
            theirs(j).wait_recv()
            near(u).wait_recv()

            def add_one(i):
                for x in (0, 1):
                    total = own_v[j * PER + i, x] + their_v[j * PER + i, x].astype(F32)
                    res_v[u * PER + i, x] = (total + near_v[u * PER + i, x].astype(F32)).astype(BF16)

            loop(PER, add_one)

        @pl.when(u > 0)
        def _():
            def send_one(i):
                s = (u - 1) * PER + i
                go_home(s, *lanes(s)[1])
                go_home(s, *lanes(s)[2])

            loop(PER, send_one)

    loop(HALF + 1, keep)

    def heard(h):
        pltpu.make_async_copy(t_heads.at[h], t_heads.at[h], temper_recv.at[h]).wait()

    loop(HEADS, heard)

    def tell(j):
        return pltpu.make_async_remote_copy(
            src_ref=t_heads,
            dst_ref=t_all.at[my_peer],
            send_sem=peer_send.at[j],
            recv_sem=peer_recv.at[my_peer],
            device_id=peer_id(j),
        )

    pltpu.make_async_copy(t_heads, t_all.at[my_peer], peer_recv.at[my_peer]).start()

    def tell_peer(j):
        @pl.when(j != my_peer)
        def _():
            tell(j).start()

    loop(PEERS, tell_peer)

    def landed(h):
        cols = head_cols(h)
        for lane, ref in enumerate((dq_ref, dk_ref, dv_ref)):
            piece = ref.at[0, :, cols]
            pltpu.make_async_copy(piece, piece, home_recv.at[lane, h]).wait()

    loop(HEADS, landed)

    def told(j):
        pltpu.make_async_copy(t_all.at[j], t_all.at[j], peer_recv.at[j]).wait()

    loop(PEERS, told)
    total = t_all[0]
    for j in range(1, PEERS):
        total = total + t_all[j]
    temper_ref[...] = total * (1.0 / (DOCS * BLOCKS * BLK))

    def sent(i):
        @pl.when(i != my_peer)
        def _():
            tell(i).wait_send()

        @pl.when(i != head)
        def _():
            temper_copy(i).wait_send()
            for lane in lanes(i):
                home_copy(i, *lane).wait_send()

    loop(HEADS, sent)

    def close(j):
        theirs(j).wait_send()

    loop(CHUNKS, close)

    def close_near(u):
        near(u).wait_send()

    loop(HALF, close_near)


def gather_grads(dq, own, oth, temper):
    hbm = pl.BlockSpec(memory_space=pl.ANY)
    vmem = pl.BlockSpec(memory_space=pltpu.VMEM)
    whole = jax.ShapeDtypeStruct((1, BLK, HEADS * HD), BF16)
    dma = pltpu.SemaphoreType.DMA
    return pl.pallas_call(
        gather_kernel,
        out_shape=(whole, whole, whole, jax.ShapeDtypeStruct((HEADS, 1, BLK), F32)),
        in_specs=[hbm, hbm, hbm, vmem],
        out_specs=(hbm, hbm, hbm, vmem),
        scratch_shapes=[
            pltpu.VMEM((CHIPS, 2, BLK, HD), F32),
            pltpu.VMEM((CHIPS, 2, BLK, HD), BF16),
            pltpu.VMEM((HEADS, 2, BLK, HD), BF16),
            pltpu.VMEM((HEADS, 2, BLK, HD), BF16),
            pltpu.VMEM((HEADS, 2, BLK, HD), BF16),
            pltpu.VMEM((HEADS, 1, BLK), F32),
            pltpu.VMEM((PEERS, HEADS, 1, BLK), F32),
            dma((CHUNKS,)),
            dma((CHUNKS,)),
            dma((CHUNKS,)),
            dma((HALF,)),
            dma((HALF,)),
            dma((3, HEADS)),
            dma((3, HEADS)),
            dma((HEADS,)),
            dma((HEADS,)),
            dma((PEERS,)),
            dma((PEERS,)),
        ],
        compiler_params=pltpu.CompilerParams(collective_id=2, has_side_effects=True),
        name="gather_grads",
    )(dq, own, oth, temper)


def settle_kernel(dq_in, dk_in, dv_in, temper_in, dq_ref, dk_ref, dv_ref, temper_ref):
    dq_ref[...] = dq_in[...]
    dk_ref[...] = dk_in[...]
    dv_ref[...] = dv_in[...]

    @pl.when(pl.program_id(0) == 0)
    def _():
        for h in range(HEADS):
            temper_ref[h] = temper_in[h, 0, 0]


def settle(dq, dk, dv, temper):
    steps = 4
    part = pl.BlockSpec((1, BLK // steps, HEADS * HD), lambda i: (0, i, 0))
    whole = jax.ShapeDtypeStruct((1, BLK, HEADS * HD), BF16)
    return pl.pallas_call(
        settle_kernel,
        grid=(steps,),
        out_shape=(whole, whole, whole, jax.ShapeDtypeStruct((HEADS,), F32)),
        in_specs=[part, part, part, pl.BlockSpec(memory_space=pltpu.VMEM)],
        out_specs=(part, part, part, pl.BlockSpec(memory_space=pltpu.SMEM)),
        name="settle",
    )(dq, dk, dv, temper)


def shards(q, k, v, g, softness, grouping, span):
    qg, kv = scatter_blocks(q, k, v, g)
    dq, own, oth, temper = attend(grouping.reshape(HEADS, BLOCKS), softness, span, qg, kv)
    return settle(*gather_grads(dq, own, oth, temper))


def solution(mesh):
    tokens = P("dp", "seq", None)
    return jax.shard_map(
        shards,
        mesh=mesh,
        in_specs=(tokens, tokens, tokens, tokens, P(), P("dp", None, None, None), P()),
        out_specs=(tokens, tokens, tokens, P()),
        check_vma=False,
    )
```

```python
import math

import jax
import jax.numpy as jnp
from jax import lax
from jax.experimental import pallas as pl
from jax.experimental.pallas import tpu as pltpu
from jax.sharding import PartitionSpec as P

HD = 128
BLK = 128
MOST = 12
NC = 8
HEADS = 16
Z = 8
CHIPS = 32
BLOCKS = 64
DOCS = 4
OFF = -1e30
F32 = jnp.float32
BF16 = jnp.bfloat16


def place():
    me = lax.axis_index("seq")
    row, col = me // (2 * Z), (me // 2) % Z
    core = me % 2
    inner = ((row + 1) // 2) % 2
    partner = me + 1 - 2 * core
    neighbour = me + 2 * Z * (1 - 2 * (row % 2))
    return me, row, col, core, inner, (row // 2) * Z + col, partner, neighbour


def row_of(half, inner):
    return half * (3 - 2 * inner) + inner


def member(i, inner, core):
    return 2 * (row_of(i // Z, inner) * Z + i % Z) + core


def loop(count, body):
    def step(i, carry):
        body(i)
        return carry

    lax.fori_loop(0, count, step, 0)


def head_cols(head):
    return pl.ds(pl.multiple_of(head * HD, HD), HD)


def in_turn(turn, col, way):
    k = turn // 2
    distance = jnp.where(k == 0, 0, jnp.where(k == 7, 4, jnp.where(k % 2 == 1, (k + 1) // 2, Z - k // 2)))
    return (turn % 2) * Z + (col + way * distance + Z) % Z


def out_turn(turn, col):
    return in_turn(HEADS - 1 - turn, col, 1)


def scatter_kernel(
    q_ref, k_ref, v_ref, g_ref, qg_ref, kv_ref, send_sem, qg_sem, kv_sem, near_send, near_recv, pass_send, pass_recv
):
    me, _, col, core, inner, head, partner, neighbour = place()
    barrier = pltpu.get_barrier_semaphore()

    def greet(i):
        @pl.when(i != head)
        def _():
            pl.semaphore_signal(barrier, inc=1, device_id={"seq": member(i, inner, core)})

    loop(HEADS, greet)
    pl.semaphore_signal(barrier, inc=1, device_id={"seq": partner})
    pl.semaphore_signal(barrier, inc=1, device_id={"seq": neighbour})
    pl.semaphore_wait(barrier, HEADS + 1)

    def pieces(h):
        cols = head_cols(h)
        return (
            (k_ref.at[0, :, cols], kv_ref.at[me, 0], kv_sem.at[head]),
            (v_ref.at[0, :, cols], kv_ref.at[me, 1], kv_sem.at[head]),
            (q_ref.at[0, :, cols], qg_ref.at[head, 0], qg_sem.at[head]),
            (g_ref.at[0, :, cols], qg_ref.at[head, 1], qg_sem.at[head]),
        )

    for src, dst, sem in pieces(head):
        pltpu.make_async_copy(src, dst, sem).start()

    def send(group, kinds):
        for kind in kinds:
            for j in (0, 2, 1, 3):
                h = in_turn(group * 4 + j, col, 1)

                @pl.when(h != head)
                def _():
                    src, dst, sem = pieces(h)[kind]
                    pltpu.make_async_remote_copy(
                        src_ref=src,
                        dst_ref=dst,
                        send_sem=send_sem.at[h],
                        recv_sem=sem,
                        device_id={"seq": member(h, inner, core)},
                    ).start()

    loop(HEADS // 4, lambda group: send(group, (0, 1)))
    loop(HEADS // 4, lambda group: send(group, (2, 3)))

    def handed(block, target, send, recv):
        return pltpu.make_async_remote_copy(
            src_ref=kv_ref.at[block],
            dst_ref=kv_ref.at[block],
            send_sem=send,
            recv_sem=recv,
            device_id={"seq": target},
        )

    def to_near(s):
        return handed(member(s, inner, core), neighbour, near_send.at[s], near_recv.at[s])

    def to_partner(s):
        return handed(member(s, inner, core), partner, pass_send.at[s], pass_recv.at[s])

    def near_to_partner(s):
        return handed(member(s, 1 - inner, core), partner, pass_send.at[HEADS + s], pass_recv.at[HEADS + s])

    def arrived(block, sem):
        pltpu.make_async_copy(kv_ref.at[block], kv_ref.at[block], sem).wait()

    lag = 2

    def take(turn):
        @pl.when(turn < HEADS)
        def _():
            s = in_turn(turn, col, -1)
            arrived(member(s, inner, core), kv_sem.at[s])
            to_near(s).start()
            to_partner(s).start()

        @pl.when(turn >= lag)
        def _():
            s = in_turn(turn - lag, col, -1)
            arrived(member(s, 1 - inner, core), near_recv.at[s])
            near_to_partner(s).start()

    loop(HEADS + lag, take)

    def finish(s):
        pltpu.make_async_copy(qg_ref.at[s], qg_ref.at[s], qg_sem.at[s]).wait()
        arrived(member(s, inner, 1 - core), pass_recv.at[s])
        arrived(member(s, 1 - inner, 1 - core), pass_recv.at[HEADS + s])
        to_near(s).wait_send()
        to_partner(s).wait_send()
        near_to_partner(s).wait_send()

        @pl.when(s != head)
        def _():
            whole = kv_ref.at[pl.ds(0, 2)]
            pltpu.make_async_copy(whole, whole, send_sem.at[s]).wait()

    loop(HEADS, finish)


def scatter_blocks(q, k, v, g):
    hbm = pl.BlockSpec(memory_space=pl.ANY)
    return pl.pallas_call(
        scatter_kernel,
        out_shape=(
            jax.ShapeDtypeStruct((HEADS, 2, BLK, HD), BF16),
            jax.ShapeDtypeStruct((BLOCKS, 2, BLK, HD), BF16),
        ),
        in_specs=[hbm] * 4,
        out_specs=(hbm, hbm),
        scratch_shapes=[pltpu.SemaphoreType.DMA((HEADS,))] * 5
        + [pltpu.SemaphoreType.DMA((2 * HEADS,))] * 2,
        compiler_params=pltpu.CompilerParams(collective_id=1, has_side_effects=True),
        name="scatter_blocks",
    )(q, k, v, g)


def dot_nt(a, b):
    return lax.dot_general(a, b, (((1,), (1,)), ((), ())), preferred_element_type=F32)


def attend_kernel(
    ids_ref,
    soft_ref,
    span_ref,
    qg_ref,
    kv_hbm,
    dq_ref,
    own_ref,
    oth_ref,
    temper_ref,
    k_sc,
    v_sc,
    kt_sc,
    dk_acc,
    dv_acc,
    s_sc,
    d_sc,
    p_sc,
    e_sc,
    t_acc,
    slot_ref,
    count_ref,
    sems,
):
    _, _, col, core, inner, head, _, _ = place()
    inverse_root = 1.0 / math.sqrt(HD)
    log2e = 1.4426950408889634
    temper = soft_ref[head]
    width = span_ref[head]
    scale = temper * inverse_root
    power = scale * log2e

    def clear(c):
        count_ref[c] = 0

    loop(NC, clear)

    def fetch(b):
        cluster = ids_ref[head, b]
        rank = count_ref[cluster]
        count_ref[cluster] = rank + 1
        slot = cluster * MOST + rank
        slot_ref[b] = slot
        rows = pl.ds(pl.multiple_of(slot * BLK, BLK), BLK)
        pltpu.make_async_copy(kv_hbm.at[b, 0], k_sc.at[rows], sems.at[0]).start()
        pltpu.make_async_copy(kv_hbm.at[b, 1], v_sc.at[rows], sems.at[1]).start()

    loop(BLOCKS, fetch)
    t_acc[...] = jnp.zeros_like(t_acc)

    def zero(i):
        rows = pl.ds(pl.multiple_of(i * BLK, BLK), BLK)
        dk_acc[rows, :] = jnp.zeros((BLK, HD), F32)
        dv_acc[rows, :] = jnp.zeros((BLK, HD), F32)

    loop(NC * MOST, zero)
    eye = (
        lax.broadcasted_iota(jnp.int32, (HD, HD), 0)
        == lax.broadcasted_iota(jnp.int32, (HD, HD), 1)
    ).astype(BF16)
    gap = lax.broadcasted_iota(jnp.int32, (BLK, BLK), 0) - lax.broadcasted_iota(
        jnp.int32, (BLK, BLK), 1
    )
    all_rows = pl.ds(0, BLOCKS * BLK)
    pltpu.make_async_copy(k_sc.at[all_rows], k_sc.at[all_rows], sems.at[0]).wait()
    pltpu.make_async_copy(v_sc.at[all_rows], v_sc.at[all_rows], sems.at[1]).wait()

    def blank(c):
        @pl.when(count_ref[c] % 2 == 1)
        def _():
            rows = pl.ds(pl.multiple_of((c * MOST + count_ref[c]) * BLK, BLK), BLK)
            k_sc[rows, :] = jnp.zeros((BLK, HD), BF16)
            v_sc[rows, :] = jnp.zeros((BLK, HD), BF16)
            kt_sc[:, rows] = jnp.zeros((HD, BLK), BF16)

    loop(NC, blank)

    def turn_keys(group):
        for j in range(8):
            start = pl.multiple_of(slot_ref[group * 8 + j] * BLK, BLK)
            kt_sc[:, pl.ds(start, BLK)] = dot_nt(eye, k_sc[pl.ds(start, BLK), :]).astype(BF16)

    loop(BLOCKS // 8, turn_keys)

    def query_block(i, block, slot, cluster, rank, blocks):
        rows = blocks * BLK
        q = qg_ref[i, 0]
        g = qg_ref[i, 1]
        first = pl.multiple_of(cluster * (MOST * BLK), BLK)
        span = pl.ds(first, rows)
        before = jnp.maximum(block - 1, 0)
        before_slot = slot_ref[before]
        usable = (block >= 1) & (before_slot // MOST != cluster)
        edge = jnp.where(usable, BLK - width, 2 * BLK)
        wstart = pl.multiple_of(before_slot * BLK, BLK)
        wspan = pl.ds(wstart, BLK)
        limit = (rank - blocks + 2) * BLK

        s_sc[pl.ds(0, rows), :] = dot_nt(k_sc[span, :], q)
        d_sc[pl.ds(0, rows), :] = dot_nt(v_sc[span, :], g)
        s_win = jnp.where(gap > edge, dot_nt(k_sc[wspan, :], q), OFF)
        s_sc[pl.ds(rows, BLK), :] = s_win
        d_sc[pl.ds(rows, BLK), :] = dot_nt(v_sc[wspan, :], g)
        for j in (blocks - 2, blocks - 1):
            part = pl.ds(j * BLK, BLK)
            shift = (j - blocks + 2) * BLK
            s_sc[part, :] = jnp.where(gap <= limit - shift, s_sc[part, :], OFF)
        top = jnp.full((8, BLK), OFF, F32)
        for j in range(blocks + 1):
            tile = s_sc[pl.ds(j * BLK, BLK), :]
            top = jnp.maximum(top, jnp.max(tile.reshape(BLK // 8, 8, BLK), axis=0))
        top = jnp.max(top, axis=0, keepdims=True)
        total = jnp.zeros((8, BLK), F32)
        mass = jnp.zeros((8, BLK), F32)
        for j in range(blocks + 1):
            part = pl.ds(j * BLK, BLK)
            weight = jnp.exp2((s_sc[part, :] - top) * power)
            p_sc[part, :] = weight
            total = total + jnp.sum(weight.reshape(BLK // 8, 8, BLK), axis=0)
            mass = mass + jnp.sum((weight * d_sc[part, :]).reshape(BLK // 8, 8, BLK), axis=0)
        inverse = 1.0 / jnp.sum(total, axis=0, keepdims=True)
        delta = jnp.sum(mass, axis=0, keepdims=True) * inverse
        terms = jnp.zeros((8, BLK), F32)
        for j in range(blocks + 1):
            part = pl.ds(j * BLK, BLK)
            prob = p_sc[part, :] * inverse
            score = prob * (d_sc[part, :] - delta)
            terms = terms + jnp.sum((score * s_sc[part, :]).reshape(BLK // 8, 8, BLK), axis=0)
            e_sc[0, part, :] = prob.astype(BF16)
            e_sc[1, part, :] = score.astype(BF16)
        t_acc[...] += terms
        body = pl.ds(0, rows)
        tail = pl.ds(rows, BLK)
        dv_acc[span, :] += jnp.dot(e_sc[0, body, :], g, preferred_element_type=F32)
        dv_acc[wspan, :] += jnp.dot(e_sc[0, tail, :], g, preferred_element_type=F32)
        dk_acc[span, :] += jnp.dot(e_sc[1, body, :], q, preferred_element_type=F32)
        dk_acc[wspan, :] += jnp.dot(e_sc[1, tail, :], q, preferred_element_type=F32)
        turned = jnp.dot(kt_sc[:, span], e_sc[1, body, :], preferred_element_type=F32)
        turned += jnp.dot(kt_sc[:, wspan], e_sc[1, tail, :], preferred_element_type=F32)
        dq_ref[i] = (turned * scale).T.astype(BF16)

    def query_step(i):
        block = member(i, inner, core)
        slot = slot_ref[block]
        cluster = slot // MOST
        rank = slot % MOST
        for blocks in range(2, MOST + 1, 2):

            @pl.when(rank // 2 == blocks // 2 - 1)
            def _():
                query_block(i, block, slot, cluster, rank, blocks)

    loop(HEADS, query_step)

    def give(i):
        at = out_turn(i % HEADS, col)
        owner = jnp.where(i < HEADS, 1 - inner, inner)
        mine = pl.ds(pl.multiple_of(slot_ref[member(at, owner, core)] * BLK, BLK), BLK)
        other = pl.ds(pl.multiple_of(slot_ref[member(at, owner, 1 - core)] * BLK, BLK), BLK)
        own_ref[i, 0] = dk_acc[mine, :] * scale
        own_ref[i, 1] = dv_acc[mine, :]
        oth_ref[i, 0] = (dk_acc[other, :] * scale).astype(BF16)
        oth_ref[i, 1] = dv_acc[other, :].astype(BF16)

    loop(CHIPS, give)
    whole = jnp.sum(jnp.sum(t_acc[...], axis=0, keepdims=True), axis=1, keepdims=True)
    temper_ref[0] = jnp.broadcast_to(whole * inverse_root, (1, BLK))


def attend(ids, soft, span, qg, kv):
    smem = pl.BlockSpec(memory_space=pltpu.SMEM)
    vmem = pl.BlockSpec(memory_space=pltpu.VMEM)
    slots = NC * MOST * BLK
    return pl.pallas_call(
        attend_kernel,
        out_shape=(
            jax.ShapeDtypeStruct((HEADS, BLK, HD), BF16),
            jax.ShapeDtypeStruct((CHIPS, 2, BLK, HD), F32),
            jax.ShapeDtypeStruct((CHIPS, 2, BLK, HD), BF16),
            jax.ShapeDtypeStruct((1, 1, BLK), F32),
        ),
        in_specs=[smem, smem, smem, vmem, pl.BlockSpec(memory_space=pl.ANY)],
        out_specs=(vmem, vmem, vmem, vmem),
        scratch_shapes=[
            pltpu.VMEM((slots, HD), BF16),
            pltpu.VMEM((slots, HD), BF16),
            pltpu.VMEM((HD, slots), BF16),
            pltpu.VMEM((slots, HD), F32),
            pltpu.VMEM((slots, HD), F32),
            pltpu.VMEM(((MOST + 1) * BLK, BLK), F32),
            pltpu.VMEM(((MOST + 1) * BLK, BLK), F32),
            pltpu.VMEM(((MOST + 1) * BLK, BLK), F32),
            pltpu.VMEM((2, (MOST + 1) * BLK, BLK), BF16),
            pltpu.VMEM((8, BLK), F32),
            pltpu.SMEM((BLOCKS,), jnp.int32),
            pltpu.SMEM((NC,), jnp.int32),
            pltpu.SemaphoreType.DMA((2,)),
        ],
        name="attend",
    )(ids, soft, span, qg, kv)


CHUNKS = 8
PER = CHIPS // CHUNKS
HALF = CHUNKS // 2
PEERS = DOCS * 4


def gather_kernel(
    dq_in,
    own_in,
    oth_in,
    temper_in,
    dq_ref,
    dk_ref,
    dv_ref,
    temper_ref,
    own_v,
    their_v,
    give_v,
    near_v,
    res_v,
    t_heads,
    t_all,
    own_sem,
    their_send,
    their_recv,
    near_send,
    near_recv,
    home_send,
    home_recv,
    temper_send,
    temper_recv,
    peer_send,
    peer_recv,
):
    me, row, col, core, inner, head, partner, neighbour = place()
    doc = lax.axis_index("dp")
    my_peer = doc * 4 + inner * 2 + core
    barrier = pltpu.get_barrier_semaphore()

    def peer_id(j):
        half = row // 2
        other = 2 * half + ((j // 2) % 2 + half) % 2
        return {"seq": 2 * (other * Z + col) + j % 2, "dp": j // 4}

    def greet_member(i):
        @pl.when(i != head)
        def _():
            pl.semaphore_signal(barrier, inc=1, device_id={"seq": member(i, inner, core)})

    loop(HEADS, greet_member)

    def greet_peer(j):
        @pl.when(j != my_peer)
        def _():
            pl.semaphore_signal(barrier, inc=1, device_id=peer_id(j))

    loop(PEERS, greet_peer)
    pl.semaphore_wait(barrier, HEADS - 1 + PEERS - 1)

    def home_copy(i, src, dst, lane):
        return pltpu.make_async_remote_copy(
            src_ref=src,
            dst_ref=dst.at[0, :, head_cols(head)],
            send_sem=home_send.at[lane, i],
            recv_sem=home_recv.at[lane, head],
            device_id={"seq": member(i, inner, core)},
        )

    def go_home(i, src, dst, lane):
        @pl.when(i != head)
        def _():
            home_copy(i, src, dst, lane).start()

        @pl.when(i == head)
        def _():
            pltpu.make_async_copy(src, dst.at[0, :, head_cols(head)], home_recv.at[lane, head]).start()

    def temper_copy(i):
        return pltpu.make_async_remote_copy(
            src_ref=temper_in.at[0],
            dst_ref=t_heads.at[head],
            send_sem=temper_send.at[i],
            recv_sem=temper_recv.at[head],
            device_id={"seq": member(i, inner, core)},
        )

    def theirs(j):
        part = pl.ds(j * PER, PER)
        return pltpu.make_async_remote_copy(
            src_ref=oth_in.at[part],
            dst_ref=their_v.at[part],
            send_sem=their_send.at[j],
            recv_sem=their_recv.at[j],
            device_id={"seq": partner},
        )

    def mine(j):
        part = pl.ds(j * PER, PER)
        return pltpu.make_async_copy(own_in.at[part], own_v.at[part], own_sem.at[j])

    def near(u):
        part = pl.ds(u * PER, PER)
        return pltpu.make_async_remote_copy(
            src_ref=give_v.at[part],
            dst_ref=near_v.at[part],
            send_sem=near_send.at[u],
            recv_sem=near_recv.at[u],
            device_id={"seq": neighbour},
        )

    def begin(j):
        theirs(j).start()
        mine(j).start()

    loop(CHUNKS, begin)
    pltpu.make_async_copy(temper_in.at[0], t_heads.at[head], temper_recv.at[head]).start()

    def send_first(group):
        for j in (0, 2, 1, 3):
            i = out_turn(group * 4 + j, col)

            @pl.when(i != head)
            def _():
                temper_copy(i).start()

            go_home(i, dq_in.at[i], dq_ref, 0)

    loop(HEADS // 4, send_first)

    def give(u):
        @pl.when(u < HALF)
        def _():
            mine(u).wait()
            theirs(u).wait_recv()

            def add_one(i):
                for x in (0, 1):
                    total = own_v[u * PER + i, x] + their_v[u * PER + i, x].astype(F32)
                    give_v[u * PER + i, x] = total.astype(BF16)

            loop(PER, add_one)

        @pl.when(u > 0)
        def _():
            near(u - 1).start()

    loop(HALF + 1, give)

    def keep(u):
        @pl.when(u < HALF)
        def _():
            mine(HALF + u).wait()
            theirs(HALF + u).wait_recv()
            near(u).wait_recv()

            def add_one(i):
                for x in (0, 1):
                    at = (HALF + u) * PER + i
                    total = own_v[at, x] + their_v[at, x].astype(F32)
                    res_v[u * PER + i, x] = (total + near_v[u * PER + i, x].astype(F32)).astype(BF16)

            loop(PER, add_one)

        @pl.when(u > 0)
        def _():
            for x in (0, 1):
                for j in (0, 2, 1, 3):
                    t = (u - 1) * PER + j
                    go_home(out_turn(t, col), res_v.at[t, x], (dk_ref, dv_ref)[x], 1 + x)

    loop(HALF + 1, keep)

    def heard(h):
        pltpu.make_async_copy(t_heads.at[h], t_heads.at[h], temper_recv.at[h]).wait()

    loop(HEADS, heard)

    def tell(j):
        return pltpu.make_async_remote_copy(
            src_ref=t_heads,
            dst_ref=t_all.at[my_peer],
            send_sem=peer_send.at[j],
            recv_sem=peer_recv.at[my_peer],
            device_id=peer_id(j),
        )

    pltpu.make_async_copy(t_heads, t_all.at[my_peer], peer_recv.at[my_peer]).start()

    def tell_peer(j):
        @pl.when(j != my_peer)
        def _():
            tell(j).start()

    loop(PEERS, tell_peer)

    def told(j):
        pltpu.make_async_copy(t_all.at[j], t_all.at[j], peer_recv.at[j]).wait()

    loop(PEERS, told)
    total = t_all[0]
    for j in range(1, PEERS):
        total = total + t_all[j]
    total = total * (1.0 / (DOCS * BLOCKS * BLK))
    for h in range(HEADS):
        temper_ref[h] = total[h, 0, 0]


    def landed(h):
        cols = head_cols(h)
        for lane, ref in enumerate((dq_ref, dk_ref, dv_ref)):
            piece = ref.at[0, :, cols]
            pltpu.make_async_copy(piece, piece, home_recv.at[lane, h]).wait()

    loop(HEADS, landed)

    def sent(i):
        @pl.when(i != my_peer)
        def _():
            tell(i).wait_send()

        @pl.when(i != head)
        def _():
            temper_copy(i).wait_send()
            for lane, dst in enumerate((dq_ref, dk_ref, dv_ref)):
                home_copy(i, dq_in.at[i], dst, lane).wait_send()

    loop(HEADS, sent)

    def close(j):
        theirs(j).wait_send()

    loop(CHUNKS, close)

    def close_near(u):
        near(u).wait_send()

    loop(HALF, close_near)


def gather_grads(dq, own, oth, temper):
    hbm = pl.BlockSpec(memory_space=pl.ANY)
    vmem = pl.BlockSpec(memory_space=pltpu.VMEM)
    whole = jax.ShapeDtypeStruct((1, BLK, HEADS * HD), BF16)
    dma = pltpu.SemaphoreType.DMA
    return pl.pallas_call(
        gather_kernel,
        out_shape=(whole, whole, whole, jax.ShapeDtypeStruct((HEADS,), F32)),
        in_specs=[hbm, hbm, hbm, vmem],
        out_specs=(hbm, hbm, hbm, pl.BlockSpec(memory_space=pltpu.SMEM)),
        scratch_shapes=[
            pltpu.VMEM((CHIPS, 2, BLK, HD), F32),
            pltpu.VMEM((CHIPS, 2, BLK, HD), BF16),
            pltpu.VMEM((HEADS, 2, BLK, HD), BF16),
            pltpu.VMEM((HEADS, 2, BLK, HD), BF16),
            pltpu.VMEM((HEADS, 2, BLK, HD), BF16),
            pltpu.VMEM((HEADS, 1, BLK), F32),
            pltpu.VMEM((PEERS, HEADS, 1, BLK), F32),
            dma((CHUNKS,)),
            dma((CHUNKS,)),
            dma((CHUNKS,)),
            dma((HALF,)),
            dma((HALF,)),
            dma((3, HEADS)),
            dma((3, HEADS)),
            dma((HEADS,)),
            dma((HEADS,)),
            dma((PEERS,)),
            dma((PEERS,)),
        ],
        compiler_params=pltpu.CompilerParams(collective_id=2, has_side_effects=True),
        name="gather_grads",
    )(dq, own, oth, temper)


PARTS = 2


def settle_kernel(dq_in, dk_in, dv_in, temper_in, dq_ref, dk_ref, dv_ref, temper_ref, hold, in_sem, out_sem):
    rows = BLK // PARTS
    pairs = ((dq_in, dq_ref), (dk_in, dk_ref), (dv_in, dv_ref))

    def take(n):
        part = pl.ds((n % PARTS) * rows, rows)
        return pltpu.make_async_copy(pairs[n // PARTS][0].at[0, part], hold.at[n], in_sem.at[n])

    def put(n):
        part = pl.ds((n % PARTS) * rows, rows)
        return pltpu.make_async_copy(hold.at[n], pairs[n // PARTS][1].at[0, part], out_sem.at[n])

    count = 3 * PARTS
    for n in range(count):
        take(n).start()
    temper_copy = pltpu.make_async_copy(temper_in, temper_ref, in_sem.at[count])
    temper_copy.start()
    for n in range(count):
        take(n).wait()
        put(n).start()
    for n in range(count):
        put(n).wait()
    temper_copy.wait()


def settle(dq, dk, dv, temper):
    hbm = pl.BlockSpec(memory_space=pl.ANY)
    whole = jax.ShapeDtypeStruct((1, BLK, HEADS * HD), BF16)
    return pl.pallas_call(
        settle_kernel,
        out_shape=(whole, whole, whole, jax.ShapeDtypeStruct((HEADS,), F32)),
        in_specs=[hbm] * 4,
        out_specs=(hbm,) * 4,
        scratch_shapes=[
            pltpu.VMEM((3 * PARTS, BLK // PARTS, HEADS * HD), BF16),
            pltpu.SemaphoreType.DMA((3 * PARTS + 1,)),
            pltpu.SemaphoreType.DMA((3 * PARTS,)),
        ],
        name="settle",
    )(dq, dk, dv, temper)


def shards(q, k, v, g, softness, grouping, span):
    qg, kv = scatter_blocks(q, k, v, g)
    dq, own, oth, temper = attend(grouping.reshape(HEADS, BLOCKS), softness, span, qg, kv)
    return settle(*gather_grads(dq, own, oth, temper))


def solution(mesh):
    tokens = P("dp", "seq", None)
    return jax.shard_map(
        shards,
        mesh=mesh,
        in_specs=(tokens, tokens, tokens, tokens, P(), P("dp", None, None, None), P()),
        out_specs=(tokens, tokens, tokens, P()),
        check_vma=False,
    )
```

```python
import math

import jax
import jax.numpy as jnp
from jax import lax
from jax.experimental import pallas as pl
from jax.experimental.pallas import tpu as pltpu
from jax.sharding import PartitionSpec as P

HD = 128
BLK = 128
MOST = 12
NC = 8
HEADS = 16
Z = 8
CHIPS = 32
BLOCKS = 64
DOCS = 4
OFF = -1e30
F32 = jnp.float32
BF16 = jnp.bfloat16


def place():
    me = lax.axis_index("seq")
    row, col = me // (2 * Z), (me // 2) % Z
    core = me % 2
    inner = ((row + 1) // 2) % 2
    partner = me + 1 - 2 * core
    neighbour = me + 2 * Z * (1 - 2 * (row % 2))
    return me, row, col, core, inner, (row // 2) * Z + col, partner, neighbour


def row_of(half, inner):
    return half * (3 - 2 * inner) + inner


def member(i, inner, core):
    return 2 * (row_of(i // Z, inner) * Z + i % Z) + core


def loop(count, body):
    def step(i, carry):
        body(i)
        return carry

    lax.fori_loop(0, count, step, 0)


def head_cols(head):
    return pl.ds(pl.multiple_of(head * HD, HD), HD)


def in_turn(turn, col, way):
    k = turn // 2
    distance = jnp.where(k == 0, 0, jnp.where(k == 7, 4, jnp.where(k % 2 == 1, (k + 1) // 2, Z - k // 2)))
    return (turn % 2) * Z + (col + way * distance + Z) % Z


def out_turn(turn, col):
    return in_turn(HEADS - 1 - turn, col, 1)


def scatter_kernel(
    q_ref, k_ref, v_ref, g_ref, qg_ref, kv_ref, send_sem, qg_sem, kv_sem, near_send, near_recv, pass_send, pass_recv
):
    me, _, col, core, inner, head, partner, neighbour = place()
    barrier = pltpu.get_barrier_semaphore()

    def greet(i):
        @pl.when(i != head)
        def _():
            pl.semaphore_signal(barrier, inc=1, device_id={"seq": member(i, inner, core)})

    loop(HEADS, greet)
    pl.semaphore_signal(barrier, inc=1, device_id={"seq": partner})
    pl.semaphore_signal(barrier, inc=1, device_id={"seq": neighbour})
    pl.semaphore_wait(barrier, HEADS + 1)

    def pieces(h):
        cols = head_cols(h)
        return (
            (k_ref.at[0, :, cols], kv_ref.at[me, 0], kv_sem.at[head]),
            (v_ref.at[0, :, cols], kv_ref.at[me, 1], kv_sem.at[head]),
            (q_ref.at[0, :, cols], qg_ref.at[head, 0], qg_sem.at[head]),
            (g_ref.at[0, :, cols], qg_ref.at[head, 1], qg_sem.at[head]),
        )

    for src, dst, sem in pieces(head):
        pltpu.make_async_copy(src, dst, sem).start()

    def send(group, kinds):
        for kind in kinds:
            for j in (0, 2, 1, 3):
                h = in_turn(group * 4 + j, col, 1)

                @pl.when(h != head)
                def _():
                    src, dst, sem = pieces(h)[kind]
                    pltpu.make_async_remote_copy(
                        src_ref=src,
                        dst_ref=dst,
                        send_sem=send_sem.at[h],
                        recv_sem=sem,
                        device_id={"seq": member(h, inner, core)},
                    ).start()

    loop(HEADS // 4, lambda group: send(group, (0, 1)))
    loop(HEADS // 4, lambda group: send(group, (2, 3)))

    def handed(block, target, send, recv):
        return pltpu.make_async_remote_copy(
            src_ref=kv_ref.at[block],
            dst_ref=kv_ref.at[block],
            send_sem=send,
            recv_sem=recv,
            device_id={"seq": target},
        )

    def to_near(s):
        return handed(member(s, inner, core), neighbour, near_send.at[s], near_recv.at[s])

    def to_partner(s):
        return handed(member(s, inner, core), partner, pass_send.at[s], pass_recv.at[s])

    def near_to_partner(s):
        return handed(member(s, 1 - inner, core), partner, pass_send.at[HEADS + s], pass_recv.at[HEADS + s])

    def arrived(block, sem):
        pltpu.make_async_copy(kv_ref.at[block], kv_ref.at[block], sem).wait()

    lag = 2

    def take(turn):
        @pl.when(turn < HEADS)
        def _():
            s = in_turn(turn, col, -1)
            arrived(member(s, inner, core), kv_sem.at[s])
            to_near(s).start()
            to_partner(s).start()

        @pl.when(turn >= lag)
        def _():
            s = in_turn(turn - lag, col, -1)
            arrived(member(s, 1 - inner, core), near_recv.at[s])
            near_to_partner(s).start()

    loop(HEADS + lag, take)

    def finish(s):
        pltpu.make_async_copy(qg_ref.at[s], qg_ref.at[s], qg_sem.at[s]).wait()
        arrived(member(s, inner, 1 - core), pass_recv.at[s])
        arrived(member(s, 1 - inner, 1 - core), pass_recv.at[HEADS + s])
        to_near(s).wait_send()
        to_partner(s).wait_send()
        near_to_partner(s).wait_send()

        @pl.when(s != head)
        def _():
            whole = kv_ref.at[pl.ds(0, 2)]
            pltpu.make_async_copy(whole, whole, send_sem.at[s]).wait()

    loop(HEADS, finish)


def scatter_blocks(q, k, v, g):
    hbm = pl.BlockSpec(memory_space=pl.ANY)
    return pl.pallas_call(
        scatter_kernel,
        out_shape=(
            jax.ShapeDtypeStruct((HEADS, 2, BLK, HD), BF16),
            jax.ShapeDtypeStruct((BLOCKS, 2, BLK, HD), BF16),
        ),
        in_specs=[hbm] * 4,
        out_specs=(hbm, hbm),
        scratch_shapes=[pltpu.SemaphoreType.DMA((HEADS,))] * 5
        + [pltpu.SemaphoreType.DMA((2 * HEADS,))] * 2,
        compiler_params=pltpu.CompilerParams(collective_id=1, has_side_effects=True),
        name="scatter_blocks",
    )(q, k, v, g)


def dot_nt(a, b):
    return lax.dot_general(a, b, (((1,), (1,)), ((), ())), preferred_element_type=F32)


def dot_tn(a, b):
    return lax.dot_general(a, b, (((0,), (0,)), ((), ())), preferred_element_type=F32)


def attend_kernel(
    ids_ref,
    soft_ref,
    span_ref,
    qg_hbm,
    kv_hbm,
    dq_hbm,
    own_hbm,
    oth_hbm,
    temper_ref,
    qg_ref,
    dq_ref,
    oth_ref,
    k_sc,
    v_sc,
    dk_acc,
    dv_acc,
    s_sc,
    d_sc,
    w_sc,
    u_sc,
    e_sc,
    top_sc,
    sum_sc,
    t_acc,
    slot_ref,
    count_ref,
    order_ref,
    place_ref,
    sems,
):
    _, _, col, core, inner, head, _, _ = place()
    inverse_root = 1.0 / math.sqrt(HD)
    log2e = 1.4426950408889634
    temper = soft_ref[head]
    width = span_ref[head]
    scale = temper * inverse_root
    power = scale * log2e

    take_qg = pltpu.make_async_copy(qg_hbm, qg_ref, sems.at[2])
    take_qg.start()

    def clear(c):
        count_ref[c] = 0

    loop(NC, clear)

    def fetch(b):
        cluster = ids_ref[head, b]
        rank = count_ref[cluster]
        count_ref[cluster] = rank + 1
        slot = cluster * MOST + rank
        slot_ref[b] = slot
        rows = pl.ds(pl.multiple_of(slot * BLK, BLK), BLK)
        pltpu.make_async_copy(kv_hbm.at[b, 0], k_sc.at[rows], sems.at[0]).start()
        pltpu.make_async_copy(kv_hbm.at[b, 1], v_sc.at[rows], sems.at[1]).start()

    loop(BLOCKS, fetch)

    def clear_rank(r):
        place_ref[r] = 0

    loop(MOST + 1, clear_rank)

    def count_rank(i):
        rank = slot_ref[member(i, inner, core)] % MOST
        place_ref[rank + 1] = place_ref[rank + 1] + 1

    loop(HEADS, count_rank)

    def add_up(r):
        place_ref[r + 1] = place_ref[r + 1] + place_ref[r]

    loop(MOST, add_up)

    def put_in_order(i):
        rank = slot_ref[member(i, inner, core)] % MOST
        at = place_ref[rank]
        order_ref[at] = i
        place_ref[rank] = at + 1

    loop(HEADS, put_in_order)
    t_acc[...] = jnp.zeros_like(t_acc)
    s_sc[...] = jnp.full_like(s_sc, OFF)
    d_sc[...] = jnp.zeros_like(d_sc)
    w_sc[...] = jnp.zeros_like(w_sc)
    u_sc[...] = jnp.zeros_like(u_sc)
    e_sc[...] = jnp.zeros_like(e_sc)
    top_sc[...] = jnp.zeros_like(top_sc)
    sum_sc[...] = jnp.zeros_like(sum_sc)

    def rows_of(block):
        return pl.ds(pl.multiple_of(slot_ref[block] * BLK, BLK), BLK)

    def zero(group):
        for j in range(4):
            rows = rows_of(group * 4 + j)
            dk_acc[rows, :] = jnp.zeros((BLK, HD), F32)
            dv_acc[rows, :] = jnp.zeros((BLK, HD), F32)

    loop(BLOCKS // 4, zero)
    gap = lax.broadcasted_iota(jnp.int32, (BLK, BLK), 0) - lax.broadcasted_iota(
        jnp.int32, (BLK, BLK), 1
    )
    all_rows = pl.ds(0, BLOCKS * BLK)
    pltpu.make_async_copy(k_sc.at[all_rows], k_sc.at[all_rows], sems.at[0]).wait()
    pltpu.make_async_copy(v_sc.at[all_rows], v_sc.at[all_rows], sems.at[1]).wait()

    def blank(c):
        def blank_slot(n):
            rows = pl.ds(pl.multiple_of((c * MOST + count_ref[c] + n) * BLK, BLK), BLK)
            k_sc[rows, :] = jnp.zeros((BLK, HD), BF16)
            v_sc[rows, :] = jnp.zeros((BLK, HD), BF16)

        loop(MOST - count_ref[c], blank_slot)

    loop(NC, blank)

    take_qg.wait()

    tail = pl.ds(MOST * BLK, BLK)

    def fold(x, how):
        return how(x.reshape(x.shape[0] // 8, 8, BLK), axis=0)

    def at_turn(n):
        i = order_ref[jnp.clip(n, 0, HEADS - 1)]
        block = member(i, inner, core)
        slot = slot_ref[block]
        before = jnp.maximum(block - 1, 0)
        return i, block, slot, before

    def spans(slot, before, blocks):
        start = pl.multiple_of(slot // MOST * (MOST * BLK), BLK)
        wstart = pl.multiple_of(slot_ref[before] * BLK, BLK)
        return pl.ds(start, blocks * BLK), pl.ds(wstart, BLK)

    def scores(n, blocks):
        i, block, slot, before = at_turn(n)
        span, wspan = spans(slot, before, blocks)
        rank = slot % MOST
        usable = (block >= 1) & (slot_ref[before] // MOST != slot // MOST)
        edge = jnp.where(usable, BLK - width, 2 * BLK)
        q = qg_ref[i, 0]
        g = qg_ref[i, 1]
        raw = dot_nt(k_sc[span, :], q)
        even = (blocks - 2) * BLK
        limit = (rank - blocks + 2) * BLK
        late = [jnp.where(gap <= limit - x * BLK, raw[even + x * BLK : even + (x + 1) * BLK], OFF) for x in (0, 1)]
        near = jnp.where(gap > edge, dot_nt(k_sc[wspan, :], q), OFF)
        top = fold(near, jnp.max)
        for part in late:
            top = jnp.maximum(top, fold(part, jnp.max))
        if even:
            s_sc[pl.ds(0, even), :] = raw[:even]
            top = jnp.maximum(top, fold(raw[:even], jnp.max))
        for x in (0, 1):
            s_sc[pl.ds(even + x * BLK, BLK), :] = late[x]
        s_sc[tail, :] = near
        top_sc[...] = top
        d_sc[pl.ds(0, blocks * BLK), :] = dot_nt(v_sc[span, :], g)
        d_sc[tail, :] = dot_nt(v_sc[wspan, :], g)

    def parts(blocks):
        starts = [j * BLK + x for j in (*range(blocks), MOST) for x in range(0, BLK, 8)]
        return [pl.ds(start, 8) for start in starts]

    def weights(blocks):
        top = jnp.max(top_sc[...], axis=0, keepdims=True)
        sums = [jnp.zeros((8, BLK), F32) for _ in range(4)]
        for part in parts(blocks):
            raw = s_sc[part, :]
            weight = jnp.exp2((raw - top) * power)
            moment = weight * d_sc[part, :]
            w_sc[part, :] = weight
            u_sc[part, :] = moment
            for x, term in enumerate((weight, moment, weight * raw, moment * raw)):
                sums[x] = sums[x] + fold(term, jnp.sum)
        for x in range(4):
            sum_sc[x] = sums[x]

    def shares(blocks):
        total, mass, weight_raw, moment_raw = [jnp.sum(sum_sc[x], axis=0, keepdims=True) for x in range(4)]
        inverse = jnp.where(total > 0.0, 1.0 / total, 0.0)
        delta = mass * inverse
        t_acc[...] += (moment_raw - delta * weight_raw) * inverse
        for part in parts(blocks):
            weight = w_sc[part, :]
            e_sc[0, part, :] = (weight * inverse).astype(BF16)
            e_sc[1, part, :] = ((u_sc[part, :] - weight * delta) * inverse).astype(BF16)

    def products(n, blocks):
        i, _, slot, before = at_turn(n)
        span, wspan = spans(slot, before, blocks)
        q = qg_ref[i, 0]
        g = qg_ref[i, 1]
        body = pl.ds(0, blocks * BLK)
        grads = dot_tn(e_sc[1, body, :], k_sc[span, :])
        grads += dot_tn(e_sc[1, tail, :], k_sc[wspan, :])
        dv_acc[span, :] += jnp.dot(e_sc[0, body, :], g, preferred_element_type=F32)
        dv_acc[wspan, :] += jnp.dot(e_sc[0, tail, :], g, preferred_element_type=F32)
        dk_acc[span, :] += jnp.dot(e_sc[1, body, :], q, preferred_element_type=F32)
        dk_acc[wspan, :] += jnp.dot(e_sc[1, tail, :], q, preferred_element_type=F32)
        dq_ref[i] = (grads * scale).astype(BF16)

    def by_size(n, work):
        rank = at_turn(n)[2] % MOST
        for blocks in range(2, MOST + 1, 2):

            @pl.when(rank // 2 == blocks // 2 - 1)
            def _():
                work(blocks)

    def step(n):
        def work(blocks):
            products(n - 3, blocks)
            shares(blocks)
            weights(blocks)
            scores(n, blocks)

        by_size(n, work)

    loop(HEADS, step)

    def drain(blocks):
        products(HEADS - 3, blocks)
        shares(blocks)
        weights(blocks)

    by_size(HEADS - 1, drain)

    def drain_more(blocks):
        products(HEADS - 2, blocks)
        shares(blocks)

    by_size(HEADS - 1, drain_more)
    by_size(HEADS - 1, lambda blocks: products(HEADS - 1, blocks))

    pltpu.make_async_copy(dq_ref, dq_hbm, sems.at[2]).start()

    def give(i):
        at = out_turn(i % HEADS, col)
        owner = jnp.where(i < HEADS, 1 - inner, inner)
        mine = rows_of(member(at, owner, core))
        other = rows_of(member(at, owner, 1 - core))
        pltpu.make_async_copy(dk_acc.at[mine], own_hbm.at[i, 0], sems.at[0]).start()
        pltpu.make_async_copy(dv_acc.at[mine], own_hbm.at[i, 1], sems.at[0]).start()
        oth_ref[i, 0] = dk_acc[other, :].astype(BF16)
        oth_ref[i, 1] = dv_acc[other, :].astype(BF16)
        pltpu.make_async_copy(oth_ref.at[i], oth_hbm.at[i], sems.at[1]).start()

    loop(CHIPS, give)
    whole = jnp.sum(t_acc[...], axis=1, keepdims=True)
    temper_ref[0] = jnp.broadcast_to(whole * inverse_root, (1, BLK))
    pltpu.make_async_copy(dq_ref, dq_hbm, sems.at[2]).wait()
    pltpu.make_async_copy(own_hbm, own_hbm, sems.at[0]).wait()
    pltpu.make_async_copy(oth_ref, oth_hbm, sems.at[1]).wait()


def attend(ids, soft, span, qg, kv):
    smem = pl.BlockSpec(memory_space=pltpu.SMEM)
    vmem = pl.BlockSpec(memory_space=pltpu.VMEM)
    hbm = pl.BlockSpec(memory_space=pl.ANY)
    slots = NC * MOST * BLK
    return pl.pallas_call(
        attend_kernel,
        out_shape=(
            jax.ShapeDtypeStruct((HEADS, BLK, HD), BF16),
            jax.ShapeDtypeStruct((CHIPS, 2, BLK, HD), F32),
            jax.ShapeDtypeStruct((CHIPS, 2, BLK, HD), BF16),
            jax.ShapeDtypeStruct((1, 1, BLK), F32),
        ),
        in_specs=[smem, smem, smem, hbm, hbm],
        out_specs=(hbm, hbm, hbm, vmem),
        scratch_shapes=[
            pltpu.VMEM((HEADS, 2, BLK, HD), BF16),
            pltpu.VMEM((HEADS, BLK, HD), BF16),
            pltpu.VMEM((CHIPS, 2, BLK, HD), BF16),
            pltpu.VMEM((slots, HD), BF16),
            pltpu.VMEM((slots, HD), BF16),
            pltpu.VMEM((slots, HD), F32),
            pltpu.VMEM((slots, HD), F32),
            pltpu.VMEM(((MOST + 1) * BLK, BLK), F32),
            pltpu.VMEM(((MOST + 1) * BLK, BLK), F32),
            pltpu.VMEM(((MOST + 1) * BLK, BLK), F32),
            pltpu.VMEM(((MOST + 1) * BLK, BLK), F32),
            pltpu.VMEM((2, (MOST + 1) * BLK, BLK), BF16),
            pltpu.VMEM((8, BLK), F32),
            pltpu.VMEM((4, 8, BLK), F32),
            pltpu.VMEM((1, BLK), F32),
            pltpu.SMEM((BLOCKS,), jnp.int32),
            pltpu.SMEM((NC,), jnp.int32),
            pltpu.SMEM((HEADS,), jnp.int32),
            pltpu.SMEM((MOST + 1,), jnp.int32),
            pltpu.SemaphoreType.DMA((3,)),
        ],
        name="attend",
    )(ids, soft, span, qg, kv)


CHUNKS = 16
PER = CHIPS // CHUNKS
HALF = CHUNKS // 2
PEERS = DOCS * 4


def gather_kernel(
    soft_ref,
    dq_in,
    own_in,
    oth_in,
    temper_in,
    dq_ref,
    dk_ref,
    dv_ref,
    temper_ref,
    own_v,
    their_v,
    give_v,
    near_v,
    res_v,
    t_heads,
    t_all,
    own_sem,
    their_send,
    their_recv,
    near_send,
    near_recv,
    home_send,
    home_recv,
    temper_send,
    temper_recv,
    peer_send,
    peer_recv,
):
    me, row, col, core, inner, head, partner, neighbour = place()
    doc = lax.axis_index("dp")
    my_peer = doc * 4 + inner * 2 + core
    scale = soft_ref[head] * (1.0 / math.sqrt(HD))
    barrier = pltpu.get_barrier_semaphore()

    def mine(j):
        part = pl.ds(j * PER, PER)
        return pltpu.make_async_copy(own_in.at[part], own_v.at[part], own_sem.at[j])

    loop(CHUNKS, lambda j: mine(j).start())

    def peer_id(j):
        half = row // 2
        other = 2 * half + ((j // 2) % 2 + half) % 2
        return {"seq": 2 * (other * Z + col) + j % 2, "dp": j // 4}

    def greet_member(i):
        @pl.when(i != head)
        def _():
            pl.semaphore_signal(barrier, inc=1, device_id={"seq": member(i, inner, core)})

    loop(HEADS, greet_member)

    def greet_peer(j):
        @pl.when(j != my_peer)
        def _():
            pl.semaphore_signal(barrier, inc=1, device_id=peer_id(j))

    loop(PEERS, greet_peer)
    pl.semaphore_wait(barrier, HEADS - 1 + PEERS - 1)

    def home_copy(i, src, dst, lane):
        return pltpu.make_async_remote_copy(
            src_ref=src,
            dst_ref=dst.at[0, :, head_cols(head)],
            send_sem=home_send.at[lane, i],
            recv_sem=home_recv.at[lane, head],
            device_id={"seq": member(i, inner, core)},
        )

    def go_home(i, src, dst, lane):
        @pl.when(i != head)
        def _():
            home_copy(i, src, dst, lane).start()

        @pl.when(i == head)
        def _():
            pltpu.make_async_copy(src, dst.at[0, :, head_cols(head)], home_recv.at[lane, head]).start()

    def temper_copy(i):
        return pltpu.make_async_remote_copy(
            src_ref=temper_in.at[0],
            dst_ref=t_heads.at[head],
            send_sem=temper_send.at[i],
            recv_sem=temper_recv.at[head],
            device_id={"seq": member(i, inner, core)},
        )

    def theirs(j):
        part = pl.ds(j * PER, PER)
        return pltpu.make_async_remote_copy(
            src_ref=oth_in.at[part],
            dst_ref=their_v.at[part],
            send_sem=their_send.at[j],
            recv_sem=their_recv.at[j],
            device_id={"seq": partner},
        )

    def near(u):
        part = pl.ds(u * PER, PER)
        return pltpu.make_async_remote_copy(
            src_ref=give_v.at[part],
            dst_ref=near_v.at[part],
            send_sem=near_send.at[u],
            recv_sem=near_recv.at[u],
            device_id={"seq": neighbour},
        )

    def begin(j):
        theirs(j).start()

    loop(CHUNKS, begin)
    pltpu.make_async_copy(temper_in.at[0], t_heads.at[head], temper_recv.at[head]).start()

    def send_first(group):
        for j in (0, 2, 1, 3):
            i = out_turn(group * 4 + j, col)

            @pl.when(i != head)
            def _():
                temper_copy(i).start()

            go_home(i, dq_in.at[i], dq_ref, 0)

    loop(HEADS // 4, send_first)

    def give(u):
        mine(u).wait()
        theirs(u).wait_recv()

        def add_one(i):
            for x in (0, 1):
                total = own_v[u * PER + i, x] + their_v[u * PER + i, x].astype(F32)
                give_v[u * PER + i, x] = total.astype(BF16)

        loop(PER, add_one)
        near(u).start()

    loop(HALF, give)

    def heard(h):
        pltpu.make_async_copy(t_heads.at[h], t_heads.at[h], temper_recv.at[h]).wait()

    loop(HEADS, heard)

    def tell(j):
        return pltpu.make_async_remote_copy(
            src_ref=t_heads,
            dst_ref=t_all.at[my_peer],
            send_sem=peer_send.at[j],
            recv_sem=peer_recv.at[my_peer],
            device_id=peer_id(j),
        )

    pltpu.make_async_copy(t_heads, t_all.at[my_peer], peer_recv.at[my_peer]).start()

    def tell_peer(j):
        @pl.when(j != my_peer)
        def _():
            tell(j).start()

    loop(PEERS, tell_peer)

    def keep(u):
        mine(HALF + u).wait()
        theirs(HALF + u).wait_recv()
        near(u).wait_recv()

        def add_one(i):
            for x in (0, 1):
                at = (HALF + u) * PER + i
                total = own_v[at, x] + their_v[at, x].astype(F32) + near_v[u * PER + i, x].astype(F32)
                res_v[u * PER + i, x] = (total * scale if x == 0 else total).astype(BF16)

        loop(PER, add_one)
        for x in (0, 1):
            for j in range(PER):
                t = u * PER + j
                go_home(out_turn(t, col), res_v.at[t, x], (dk_ref, dv_ref)[x], 1 + x)

    loop(HALF, keep)

    def told(j):
        pltpu.make_async_copy(t_all.at[j], t_all.at[j], peer_recv.at[j]).wait()

    loop(PEERS, told)
    total = t_all[0]
    for j in range(1, PEERS):
        total = total + t_all[j]
    total = total * (1.0 / (DOCS * BLOCKS * BLK))
    for h in range(HEADS):
        temper_ref[h] = total[h, 0, 0]


    def landed(h):
        cols = head_cols(h)
        for lane, ref in enumerate((dq_ref, dk_ref, dv_ref)):
            piece = ref.at[0, :, cols]
            pltpu.make_async_copy(piece, piece, home_recv.at[lane, h]).wait()

    loop(HEADS, landed)

    def sent(i):
        @pl.when(i != my_peer)
        def _():
            tell(i).wait_send()

        @pl.when(i != head)
        def _():
            temper_copy(i).wait_send()
            for lane, dst in enumerate((dq_ref, dk_ref, dv_ref)):
                home_copy(i, dq_in.at[i], dst, lane).wait_send()

    loop(HEADS, sent)

    def close(j):
        theirs(j).wait_send()

    loop(CHUNKS, close)

    def close_near(u):
        near(u).wait_send()

    loop(HALF, close_near)


def gather_grads(soft, dq, own, oth, temper):
    hbm = pl.BlockSpec(memory_space=pl.ANY)
    vmem = pl.BlockSpec(memory_space=pltpu.VMEM)
    whole = jax.ShapeDtypeStruct((1, BLK, HEADS * HD), BF16)
    dma = pltpu.SemaphoreType.DMA
    return pl.pallas_call(
        gather_kernel,
        out_shape=(whole, whole, whole, jax.ShapeDtypeStruct((HEADS,), F32)),
        in_specs=[pl.BlockSpec(memory_space=pltpu.SMEM), hbm, hbm, hbm, vmem],
        out_specs=(hbm, hbm, hbm, pl.BlockSpec(memory_space=pltpu.SMEM)),
        scratch_shapes=[
            pltpu.VMEM((CHIPS, 2, BLK, HD), F32),
            pltpu.VMEM((CHIPS, 2, BLK, HD), BF16),
            pltpu.VMEM((HEADS, 2, BLK, HD), BF16),
            pltpu.VMEM((HEADS, 2, BLK, HD), BF16),
            pltpu.VMEM((HEADS, 2, BLK, HD), BF16),
            pltpu.VMEM((HEADS, 1, BLK), F32),
            pltpu.VMEM((PEERS, HEADS, 1, BLK), F32),
            dma((CHUNKS,)),
            dma((CHUNKS,)),
            dma((CHUNKS,)),
            dma((HALF,)),
            dma((HALF,)),
            dma((3, HEADS)),
            dma((3, HEADS)),
            dma((HEADS,)),
            dma((HEADS,)),
            dma((PEERS,)),
            dma((PEERS,)),
        ],
        compiler_params=pltpu.CompilerParams(collective_id=2, has_side_effects=True),
        name="gather_grads",
    )(soft, dq, own, oth, temper)


PARTS = 2


def settle_kernel(dq_in, dk_in, dv_in, temper_in, dq_ref, dk_ref, dv_ref, temper_ref, hold, in_sem, out_sem):
    rows = BLK // PARTS
    pairs = ((dq_in, dq_ref), (dk_in, dk_ref), (dv_in, dv_ref))

    def take(n):
        part = pl.ds((n % PARTS) * rows, rows)
        return pltpu.make_async_copy(pairs[n // PARTS][0].at[0, part], hold.at[n], in_sem.at[n])

    def put(n):
        part = pl.ds((n % PARTS) * rows, rows)
        return pltpu.make_async_copy(hold.at[n], pairs[n // PARTS][1].at[0, part], out_sem.at[n])

    count = 3 * PARTS
    for n in range(count):
        take(n).start()
    temper_copy = pltpu.make_async_copy(temper_in, temper_ref, in_sem.at[count])
    temper_copy.start()
    for n in range(count):
        take(n).wait()
        put(n).start()
    for n in range(count):
        put(n).wait()
    temper_copy.wait()


def settle(dq, dk, dv, temper):
    hbm = pl.BlockSpec(memory_space=pl.ANY)
    whole = jax.ShapeDtypeStruct((1, BLK, HEADS * HD), BF16)
    return pl.pallas_call(
        settle_kernel,
        out_shape=(whole, whole, whole, jax.ShapeDtypeStruct((HEADS,), F32)),
        in_specs=[hbm] * 4,
        out_specs=(hbm,) * 4,
        scratch_shapes=[
            pltpu.VMEM((3 * PARTS, BLK // PARTS, HEADS * HD), BF16),
            pltpu.SemaphoreType.DMA((3 * PARTS + 1,)),
            pltpu.SemaphoreType.DMA((3 * PARTS,)),
        ],
        name="settle",
    )(dq, dk, dv, temper)


def shards(q, k, v, g, softness, grouping, span):
    qg, kv = scatter_blocks(q, k, v, g)
    dq, own, oth, temper = attend(grouping.reshape(HEADS, BLOCKS), softness, span, qg, kv)
    return settle(*gather_grads(softness, dq, own, oth, temper))


def solution(mesh):
    tokens = P("dp", "seq", None)
    return jax.shard_map(
        shards,
        mesh=mesh,
        in_specs=(tokens, tokens, tokens, tokens, P(), P("dp", None, None, None), P()),
        out_specs=(tokens, tokens, tokens, P()),
        check_vma=False,
    )
```

```python
import math

import jax
import jax.numpy as jnp
from jax import lax
from jax.experimental import pallas as pl
from jax.experimental.pallas import tpu as pltpu
from jax.sharding import PartitionSpec as P

HD = 128
BLK = 128
MOST = 12
NC = 8
HEADS = 16
Z = 8
CHIPS = 32
BLOCKS = 64
DOCS = 4
OFF = -1e30
F32 = jnp.float32
BF16 = jnp.bfloat16


def place():
    me = lax.axis_index("seq")
    row, col = me // (2 * Z), (me // 2) % Z
    core = me % 2
    inner = ((row + 1) // 2) % 2
    partner = me + 1 - 2 * core
    neighbour = me + 2 * Z * (1 - 2 * (row % 2))
    return me, row, col, core, inner, (row // 2) * Z + col, partner, neighbour


def row_of(half, inner):
    return half * (3 - 2 * inner) + inner


def member(i, inner, core):
    return 2 * (row_of(i // Z, inner) * Z + i % Z) + core


def loop(count, body):
    def step(i, carry):
        body(i)
        return carry

    lax.fori_loop(0, count, step, 0)


def head_cols(head):
    return pl.ds(pl.multiple_of(head * HD, HD), HD)


def in_turn(turn, col, way):
    k = turn // 2
    distance = jnp.where(k == 0, 0, jnp.where(k == 7, 4, jnp.where(k % 2 == 1, (k + 1) // 2, Z - k // 2)))
    return (turn % 2) * Z + (col + way * distance + Z) % Z


def out_turn(turn, col):
    return in_turn(HEADS - 1 - turn, col, 1)


def scatter_kernel(
    q_ref, k_ref, v_ref, g_ref, qg_ref, kv_ref, send_sem, qg_sem, kv_sem, near_send, near_recv, pass_send, pass_recv
):
    me, _, col, core, inner, head, partner, neighbour = place()
    barrier = pltpu.get_barrier_semaphore()

    def greet(i):
        @pl.when(i != head)
        def _():
            pl.semaphore_signal(barrier, inc=1, device_id={"seq": member(i, inner, core)})

    loop(HEADS, greet)
    pl.semaphore_signal(barrier, inc=1, device_id={"seq": partner})
    pl.semaphore_signal(barrier, inc=1, device_id={"seq": neighbour})
    pl.semaphore_wait(barrier, HEADS + 1)

    def pieces(h):
        cols = head_cols(h)
        return (
            (k_ref.at[0, :, cols], kv_ref.at[me, 0], kv_sem.at[head]),
            (v_ref.at[0, :, cols], kv_ref.at[me, 1], kv_sem.at[head]),
            (q_ref.at[0, :, cols], qg_ref.at[head, 0], qg_sem.at[head]),
            (g_ref.at[0, :, cols], qg_ref.at[head, 1], qg_sem.at[head]),
        )

    for src, dst, sem in pieces(head):
        pltpu.make_async_copy(src, dst, sem).start()

    def send(group, kinds):
        for kind in kinds:
            for j in (0, 2, 1, 3):
                h = in_turn(group * 4 + j, col, 1)

                @pl.when(h != head)
                def _():
                    src, dst, sem = pieces(h)[kind]
                    pltpu.make_async_remote_copy(
                        src_ref=src,
                        dst_ref=dst,
                        send_sem=send_sem.at[h],
                        recv_sem=sem,
                        device_id={"seq": member(h, inner, core)},
                    ).start()

    loop(HEADS // 4, lambda group: send(group, (0, 1)))
    loop(HEADS // 4, lambda group: send(group, (2, 3)))

    def handed(block, target, send, recv):
        return pltpu.make_async_remote_copy(
            src_ref=kv_ref.at[block],
            dst_ref=kv_ref.at[block],
            send_sem=send,
            recv_sem=recv,
            device_id={"seq": target},
        )

    def to_near(s):
        return handed(member(s, inner, core), neighbour, near_send.at[s], near_recv.at[s])

    def to_partner(s):
        return handed(member(s, inner, core), partner, pass_send.at[s], pass_recv.at[s])

    def near_to_partner(s):
        return handed(member(s, 1 - inner, core), partner, pass_send.at[HEADS + s], pass_recv.at[HEADS + s])

    def arrived(block, sem):
        pltpu.make_async_copy(kv_ref.at[block], kv_ref.at[block], sem).wait()

    lag = 2

    def take(turn):
        @pl.when(turn < HEADS)
        def _():
            s = in_turn(turn, col, -1)
            arrived(member(s, inner, core), kv_sem.at[s])
            to_near(s).start()
            to_partner(s).start()

        @pl.when(turn >= lag)
        def _():
            s = in_turn(turn - lag, col, -1)
            arrived(member(s, 1 - inner, core), near_recv.at[s])
            near_to_partner(s).start()

    loop(HEADS + lag, take)

    def finish(s):
        pltpu.make_async_copy(qg_ref.at[s], qg_ref.at[s], qg_sem.at[s]).wait()
        arrived(member(s, inner, 1 - core), pass_recv.at[s])
        arrived(member(s, 1 - inner, 1 - core), pass_recv.at[HEADS + s])
        to_near(s).wait_send()
        to_partner(s).wait_send()
        near_to_partner(s).wait_send()

        @pl.when(s != head)
        def _():
            whole = kv_ref.at[pl.ds(0, 2)]
            pltpu.make_async_copy(whole, whole, send_sem.at[s]).wait()

    loop(HEADS, finish)


def scatter_blocks(q, k, v, g):
    hbm = pl.BlockSpec(memory_space=pl.ANY)
    return pl.pallas_call(
        scatter_kernel,
        out_shape=(
            jax.ShapeDtypeStruct((HEADS, 2, BLK, HD), BF16),
            jax.ShapeDtypeStruct((BLOCKS, 2, BLK, HD), BF16),
        ),
        in_specs=[hbm] * 4,
        out_specs=(hbm, hbm),
        scratch_shapes=[pltpu.SemaphoreType.DMA((HEADS,))] * 5
        + [pltpu.SemaphoreType.DMA((2 * HEADS,))] * 2,
        compiler_params=pltpu.CompilerParams(collective_id=1, has_side_effects=True),
        name="scatter_blocks",
    )(q, k, v, g)


def dot_nt(a, b):
    return lax.dot_general(a, b, (((1,), (1,)), ((), ())), preferred_element_type=F32)


def dot_tn(a, b):
    return lax.dot_general(a, b, (((0,), (0,)), ((), ())), preferred_element_type=F32)


def attend_kernel(
    ids_ref,
    soft_ref,
    span_ref,
    qg_hbm,
    kv_hbm,
    dq_hbm,
    own_hbm,
    oth_hbm,
    temper_ref,
    qg_ref,
    dq_ref,
    oth_ref,
    k_sc,
    v_sc,
    dk_acc,
    dv_acc,
    s_sc,
    d_sc,
    w_sc,
    u_sc,
    e_sc,
    top_sc,
    sum_sc,
    t_acc,
    slot_ref,
    count_ref,
    order_ref,
    place_ref,
    sems,
):
    _, _, col, core, inner, head, _, _ = place()
    inverse_root = 1.0 / math.sqrt(HD)
    log2e = 1.4426950408889634
    temper = soft_ref[head]
    width = span_ref[head]
    scale = temper * inverse_root
    power = scale * log2e

    take_qg = pltpu.make_async_copy(qg_hbm, qg_ref, sems.at[2])
    take_qg.start()

    def clear(c):
        count_ref[c] = 0

    loop(NC, clear)

    def fetch(b):
        cluster = ids_ref[head, b]
        rank = count_ref[cluster]
        count_ref[cluster] = rank + 1
        slot = cluster * MOST + rank
        slot_ref[b] = slot
        rows = pl.ds(pl.multiple_of(slot * BLK, BLK), BLK)
        pltpu.make_async_copy(kv_hbm.at[b, 0], k_sc.at[rows], sems.at[0]).start()
        pltpu.make_async_copy(kv_hbm.at[b, 1], v_sc.at[rows], sems.at[1]).start()
        dk_acc[rows, :] = jnp.zeros((BLK, HD), F32)
        dv_acc[rows, :] = jnp.zeros((BLK, HD), F32)
        part = pl.ds(pl.multiple_of(jnp.minimum(b, (MOST + 1) * BLK // 32 - 1) * 32, 32), 32)
        s_sc[part, :] = jnp.full((32, BLK), OFF, F32)
        for ref in (d_sc, w_sc, u_sc):
            ref[part, :] = jnp.zeros((32, BLK), F32)
        for x in (0, 1):
            e_sc[x, part, :] = jnp.zeros((32, BLK), BF16)

    loop(BLOCKS, fetch)

    def clear_rank(r):
        place_ref[r] = 0

    loop(MOST + 1, clear_rank)

    def count_rank(i):
        rank = slot_ref[member(i, inner, core)] % MOST
        place_ref[rank + 1] = place_ref[rank + 1] + 1

    loop(HEADS, count_rank)

    def add_up(r):
        place_ref[r + 1] = place_ref[r + 1] + place_ref[r]

    loop(MOST, add_up)

    def put_in_order(i):
        rank = slot_ref[member(i, inner, core)] % MOST
        at = place_ref[rank]
        order_ref[at] = i
        place_ref[rank] = at + 1

    loop(HEADS, put_in_order)
    t_acc[...] = jnp.zeros_like(t_acc)
    top_sc[...] = jnp.zeros_like(top_sc)
    sum_sc[...] = jnp.zeros_like(sum_sc)

    def rows_of(block):
        return pl.ds(pl.multiple_of(slot_ref[block] * BLK, BLK), BLK)

    gap = lax.broadcasted_iota(jnp.int32, (BLK, BLK), 0) - lax.broadcasted_iota(
        jnp.int32, (BLK, BLK), 1
    )
    all_rows = pl.ds(0, BLOCKS * BLK)
    pltpu.make_async_copy(k_sc.at[all_rows], k_sc.at[all_rows], sems.at[0]).wait()
    pltpu.make_async_copy(v_sc.at[all_rows], v_sc.at[all_rows], sems.at[1]).wait()

    def blank(c):
        def blank_slot(n):
            rows = pl.ds(pl.multiple_of((c * MOST + count_ref[c] + n) * BLK, BLK), BLK)
            k_sc[rows, :] = jnp.zeros((BLK, HD), BF16)
            v_sc[rows, :] = jnp.zeros((BLK, HD), BF16)

        loop(MOST - count_ref[c], blank_slot)

    loop(NC, blank)

    take_qg.wait()

    tail = pl.ds(MOST * BLK, BLK)

    def fold(x, how):
        return how(x.reshape(x.shape[0] // 8, 8, BLK), axis=0)

    def at_turn(n):
        i = order_ref[jnp.clip(n, 0, HEADS - 1)]
        block = member(i, inner, core)
        slot = slot_ref[block]
        before = jnp.maximum(block - 1, 0)
        return i, block, slot, before

    def spans(slot, before, blocks):
        start = pl.multiple_of(slot // MOST * (MOST * BLK), BLK)
        wstart = pl.multiple_of(slot_ref[before] * BLK, BLK)
        return pl.ds(start, blocks * BLK), pl.ds(wstart, BLK)

    def scores(n, blocks):
        i, block, slot, before = at_turn(n)
        span, wspan = spans(slot, before, blocks)
        rank = slot % MOST
        usable = (block >= 1) & (slot_ref[before] // MOST != slot // MOST)
        edge = jnp.where(usable, BLK - width, 2 * BLK)
        q = qg_ref[i, 0]
        g = qg_ref[i, 1]
        raw = dot_nt(k_sc[span, :], q)
        even = (blocks - 2) * BLK
        limit = (rank - blocks + 2) * BLK
        late = [jnp.where(gap <= limit - x * BLK, raw[even + x * BLK : even + (x + 1) * BLK], OFF) for x in (0, 1)]
        near = jnp.where(gap > edge, dot_nt(k_sc[wspan, :], q), OFF)
        top = fold(near, jnp.max)
        for part in late:
            top = jnp.maximum(top, fold(part, jnp.max))
        if even:
            s_sc[pl.ds(0, even), :] = raw[:even]
            top = jnp.maximum(top, fold(raw[:even], jnp.max))
        for x in (0, 1):
            s_sc[pl.ds(even + x * BLK, BLK), :] = late[x]
        s_sc[tail, :] = near
        top_sc[...] = top
        d_sc[pl.ds(0, blocks * BLK), :] = dot_nt(v_sc[span, :], g)
        d_sc[tail, :] = dot_nt(v_sc[wspan, :], g)

    def parts(blocks):
        starts = [j * BLK + x for j in (*range(blocks), MOST) for x in range(0, BLK, 8)]
        return [pl.ds(start, 8) for start in starts]

    def weights(blocks):
        top = jnp.max(top_sc[...], axis=0, keepdims=True)
        sums = [jnp.zeros((8, BLK), F32) for _ in range(4)]
        for part in parts(blocks):
            raw = s_sc[part, :]
            weight = jnp.exp2((raw - top) * power)
            moment = weight * d_sc[part, :]
            w_sc[part, :] = weight
            u_sc[part, :] = moment
            for x, term in enumerate((weight, moment, weight * raw, moment * raw)):
                sums[x] = sums[x] + fold(term, jnp.sum)
        for x in range(4):
            sum_sc[x] = sums[x]

    def shares(blocks):
        total, mass, weight_raw, moment_raw = [jnp.sum(sum_sc[x], axis=0, keepdims=True) for x in range(4)]
        inverse = jnp.where(total > 0.0, 1.0 / total, 0.0)
        delta = mass * inverse
        t_acc[...] += (moment_raw - delta * weight_raw) * inverse
        for part in parts(blocks):
            weight = w_sc[part, :]
            e_sc[0, part, :] = (weight * inverse).astype(BF16)
            e_sc[1, part, :] = ((u_sc[part, :] - weight * delta) * inverse).astype(BF16)

    def products(n, blocks):
        i, _, slot, before = at_turn(n)
        span, wspan = spans(slot, before, blocks)
        q = qg_ref[i, 0]
        g = qg_ref[i, 1]
        body = pl.ds(0, blocks * BLK)
        grads = dot_tn(e_sc[1, body, :], k_sc[span, :])
        grads += dot_tn(e_sc[1, tail, :], k_sc[wspan, :])
        dv_acc[span, :] += jnp.dot(e_sc[0, body, :], g, preferred_element_type=F32)
        dv_acc[wspan, :] += jnp.dot(e_sc[0, tail, :], g, preferred_element_type=F32)
        dk_acc[span, :] += jnp.dot(e_sc[1, body, :], q, preferred_element_type=F32)
        dk_acc[wspan, :] += jnp.dot(e_sc[1, tail, :], q, preferred_element_type=F32)
        dq_ref[i] = (grads * scale).astype(BF16)

    def by_size(n, work):
        rank = at_turn(n)[2] % MOST
        for blocks in range(2, MOST + 1, 2):

            @pl.when(rank // 2 == blocks // 2 - 1)
            def _():
                work(blocks)

    def step(n):
        def work(blocks):
            products(n - 3, blocks)
            shares(blocks)
            weights(blocks)
            scores(n, blocks)

        by_size(n, work)

    loop(HEADS, step)

    def drain(blocks):
        products(HEADS - 3, blocks)
        shares(blocks)
        weights(blocks)

    by_size(HEADS - 1, drain)

    def drain_more(blocks):
        products(HEADS - 2, blocks)
        shares(blocks)

    by_size(HEADS - 1, drain_more)
    by_size(HEADS - 1, lambda blocks: products(HEADS - 1, blocks))

    pltpu.make_async_copy(dq_ref, dq_hbm, sems.at[2]).start()

    def give(i):
        at = out_turn(i % HEADS, col)
        owner = jnp.where(i < HEADS, 1 - inner, inner)
        mine = rows_of(member(at, owner, core))
        other = rows_of(member(at, owner, 1 - core))
        pltpu.make_async_copy(dk_acc.at[mine], own_hbm.at[i, 0], sems.at[0]).start()
        pltpu.make_async_copy(dv_acc.at[mine], own_hbm.at[i, 1], sems.at[0]).start()
        oth_ref[i, 0] = dk_acc[other, :].astype(BF16)
        oth_ref[i, 1] = dv_acc[other, :].astype(BF16)
        pltpu.make_async_copy(oth_ref.at[i], oth_hbm.at[i], sems.at[1]).start()

    loop(CHIPS, give)
    whole = jnp.sum(t_acc[...], axis=1, keepdims=True)
    temper_ref[0] = jnp.broadcast_to(whole * inverse_root, (1, BLK))
    pltpu.make_async_copy(dq_ref, dq_hbm, sems.at[2]).wait()
    pltpu.make_async_copy(own_hbm, own_hbm, sems.at[0]).wait()
    pltpu.make_async_copy(oth_ref, oth_hbm, sems.at[1]).wait()


def attend(ids, soft, span, qg, kv):
    smem = pl.BlockSpec(memory_space=pltpu.SMEM)
    vmem = pl.BlockSpec(memory_space=pltpu.VMEM)
    hbm = pl.BlockSpec(memory_space=pl.ANY)
    slots = NC * MOST * BLK
    return pl.pallas_call(
        attend_kernel,
        out_shape=(
            jax.ShapeDtypeStruct((HEADS, BLK, HD), BF16),
            jax.ShapeDtypeStruct((CHIPS, 2, BLK, HD), F32),
            jax.ShapeDtypeStruct((CHIPS, 2, BLK, HD), BF16),
            jax.ShapeDtypeStruct((1, 1, BLK), F32),
        ),
        in_specs=[smem, smem, smem, hbm, hbm],
        out_specs=(hbm, hbm, hbm, vmem),
        scratch_shapes=[
            pltpu.VMEM((HEADS, 2, BLK, HD), BF16),
            pltpu.VMEM((HEADS, BLK, HD), BF16),
            pltpu.VMEM((CHIPS, 2, BLK, HD), BF16),
            pltpu.VMEM((slots, HD), BF16),
            pltpu.VMEM((slots, HD), BF16),
            pltpu.VMEM((slots, HD), F32),
            pltpu.VMEM((slots, HD), F32),
            pltpu.VMEM(((MOST + 1) * BLK, BLK), F32),
            pltpu.VMEM(((MOST + 1) * BLK, BLK), F32),
            pltpu.VMEM(((MOST + 1) * BLK, BLK), F32),
            pltpu.VMEM(((MOST + 1) * BLK, BLK), F32),
            pltpu.VMEM((2, (MOST + 1) * BLK, BLK), BF16),
            pltpu.VMEM((8, BLK), F32),
            pltpu.VMEM((4, 8, BLK), F32),
            pltpu.VMEM((1, BLK), F32),
            pltpu.SMEM((BLOCKS,), jnp.int32),
            pltpu.SMEM((NC,), jnp.int32),
            pltpu.SMEM((HEADS,), jnp.int32),
            pltpu.SMEM((MOST + 1,), jnp.int32),
            pltpu.SemaphoreType.DMA((3,)),
        ],
        name="attend",
    )(ids, soft, span, qg, kv)


CHUNKS = 16
PER = CHIPS // CHUNKS
HALF = CHUNKS // 2
PEERS = DOCS * 4


def gather_kernel(
    soft_ref,
    dq_in,
    own_in,
    oth_in,
    temper_in,
    dq_ref,
    dk_ref,
    dv_ref,
    temper_ref,
    own_v,
    their_v,
    give_v,
    near_v,
    res_v,
    t_heads,
    t_all,
    own_sem,
    their_send,
    their_recv,
    near_send,
    near_recv,
    home_send,
    home_recv,
    temper_send,
    temper_recv,
    peer_send,
    peer_recv,
):
    me, row, col, core, inner, head, partner, neighbour = place()
    doc = lax.axis_index("dp")
    my_peer = doc * 4 + inner * 2 + core
    scale = soft_ref[head] * (1.0 / math.sqrt(HD))
    barrier = pltpu.get_barrier_semaphore()

    def mine(j):
        part = pl.ds(j * PER, PER)
        return pltpu.make_async_copy(own_in.at[part], own_v.at[part], own_sem.at[j])

    loop(CHUNKS, lambda j: mine(j).start())

    def peer_id(j):
        half = row // 2
        other = 2 * half + ((j // 2) % 2 + half) % 2
        return {"seq": 2 * (other * Z + col) + j % 2, "dp": j // 4}

    def greet_member(i):
        @pl.when(i != head)
        def _():
            pl.semaphore_signal(barrier, inc=1, device_id={"seq": member(i, inner, core)})

    loop(HEADS, greet_member)

    def greet_peer(j):
        @pl.when(j != my_peer)
        def _():
            pl.semaphore_signal(barrier, inc=1, device_id=peer_id(j))

    loop(PEERS, greet_peer)
    pl.semaphore_wait(barrier, HEADS - 1 + PEERS - 1)

    def home_copy(i, src, dst, lane):
        return pltpu.make_async_remote_copy(
            src_ref=src,
            dst_ref=dst.at[0, :, head_cols(head)],
            send_sem=home_send.at[lane, i],
            recv_sem=home_recv.at[lane, head],
            device_id={"seq": member(i, inner, core)},
        )

    def go_home(i, src, dst, lane):
        @pl.when(i != head)
        def _():
            home_copy(i, src, dst, lane).start()

        @pl.when(i == head)
        def _():
            pltpu.make_async_copy(src, dst.at[0, :, head_cols(head)], home_recv.at[lane, head]).start()

    def temper_copy(i):
        return pltpu.make_async_remote_copy(
            src_ref=temper_in.at[0],
            dst_ref=t_heads.at[head],
            send_sem=temper_send.at[i],
            recv_sem=temper_recv.at[head],
            device_id={"seq": member(i, inner, core)},
        )

    def theirs(j):
        part = pl.ds(j * PER, PER)
        return pltpu.make_async_remote_copy(
            src_ref=oth_in.at[part],
            dst_ref=their_v.at[part],
            send_sem=their_send.at[j],
            recv_sem=their_recv.at[j],
            device_id={"seq": partner},
        )

    def near(u):
        part = pl.ds(u * PER, PER)
        return pltpu.make_async_remote_copy(
            src_ref=give_v.at[part],
            dst_ref=near_v.at[part],
            send_sem=near_send.at[u],
            recv_sem=near_recv.at[u],
            device_id={"seq": neighbour},
        )

    def begin(j):
        theirs(j).start()

    loop(CHUNKS, begin)
    pltpu.make_async_copy(temper_in.at[0], t_heads.at[head], temper_recv.at[head]).start()

    def send_first(group):
        for j in (0, 2, 1, 3):
            i = out_turn(group * 4 + j, col)

            @pl.when(i != head)
            def _():
                temper_copy(i).start()

            go_home(i, dq_in.at[i], dq_ref, 0)

    loop(HEADS // 4, send_first)

    def give(u):
        mine(u).wait()
        theirs(u).wait_recv()

        def add_one(i):
            for x in (0, 1):
                total = own_v[u * PER + i, x] + their_v[u * PER + i, x].astype(F32)
                give_v[u * PER + i, x] = total.astype(BF16)

        loop(PER, add_one)
        near(u).start()

    loop(HALF, give)

    def heard(h):
        pltpu.make_async_copy(t_heads.at[h], t_heads.at[h], temper_recv.at[h]).wait()

    loop(HEADS, heard)

    def tell(j):
        return pltpu.make_async_remote_copy(
            src_ref=t_heads,
            dst_ref=t_all.at[my_peer],
            send_sem=peer_send.at[j],
            recv_sem=peer_recv.at[my_peer],
            device_id=peer_id(j),
        )

    pltpu.make_async_copy(t_heads, t_all.at[my_peer], peer_recv.at[my_peer]).start()

    def tell_peer(j):
        @pl.when(j != my_peer)
        def _():
            tell(j).start()

    loop(PEERS, tell_peer)

    def keep(u):
        mine(HALF + u).wait()
        theirs(HALF + u).wait_recv()
        near(u).wait_recv()

        def add_one(i):
            for x in (0, 1):
                at = (HALF + u) * PER + i
                total = own_v[at, x] + their_v[at, x].astype(F32) + near_v[u * PER + i, x].astype(F32)
                res_v[u * PER + i, x] = (total * scale if x == 0 else total).astype(BF16)

        loop(PER, add_one)
        for x in (0, 1):
            for j in range(PER):
                t = u * PER + j
                go_home(out_turn(t, col), res_v.at[t, x], (dk_ref, dv_ref)[x], 1 + x)

    loop(HALF, keep)

    def told(j):
        pltpu.make_async_copy(t_all.at[j], t_all.at[j], peer_recv.at[j]).wait()

    loop(PEERS, told)
    total = t_all[0]
    for j in range(1, PEERS):
        total = total + t_all[j]
    total = total * (1.0 / (DOCS * BLOCKS * BLK))
    for h in range(HEADS):
        temper_ref[h] = total[h, 0, 0]


    def landed(h):
        cols = head_cols(h)
        for lane, ref in enumerate((dq_ref, dk_ref, dv_ref)):
            piece = ref.at[0, :, cols]
            pltpu.make_async_copy(piece, piece, home_recv.at[lane, h]).wait()

    loop(HEADS, landed)

    def sent(i):
        @pl.when(i != my_peer)
        def _():
            tell(i).wait_send()

        @pl.when(i != head)
        def _():
            temper_copy(i).wait_send()
            for lane, dst in enumerate((dq_ref, dk_ref, dv_ref)):
                home_copy(i, dq_in.at[i], dst, lane).wait_send()

    loop(HEADS, sent)

    def close(j):
        theirs(j).wait_send()

    loop(CHUNKS, close)

    def close_near(u):
        near(u).wait_send()

    loop(HALF, close_near)


def gather_grads(soft, dq, own, oth, temper):
    hbm = pl.BlockSpec(memory_space=pl.ANY)
    vmem = pl.BlockSpec(memory_space=pltpu.VMEM)
    whole = jax.ShapeDtypeStruct((1, BLK, HEADS * HD), BF16)
    dma = pltpu.SemaphoreType.DMA
    return pl.pallas_call(
        gather_kernel,
        out_shape=(whole, whole, whole, jax.ShapeDtypeStruct((HEADS,), F32)),
        in_specs=[pl.BlockSpec(memory_space=pltpu.SMEM), hbm, hbm, hbm, vmem],
        out_specs=(hbm, hbm, hbm, pl.BlockSpec(memory_space=pltpu.SMEM)),
        scratch_shapes=[
            pltpu.VMEM((CHIPS, 2, BLK, HD), F32),
            pltpu.VMEM((CHIPS, 2, BLK, HD), BF16),
            pltpu.VMEM((HEADS, 2, BLK, HD), BF16),
            pltpu.VMEM((HEADS, 2, BLK, HD), BF16),
            pltpu.VMEM((HEADS, 2, BLK, HD), BF16),
            pltpu.VMEM((HEADS, 1, BLK), F32),
            pltpu.VMEM((PEERS, HEADS, 1, BLK), F32),
            dma((CHUNKS,)),
            dma((CHUNKS,)),
            dma((CHUNKS,)),
            dma((HALF,)),
            dma((HALF,)),
            dma((3, HEADS)),
            dma((3, HEADS)),
            dma((HEADS,)),
            dma((HEADS,)),
            dma((PEERS,)),
            dma((PEERS,)),
        ],
        compiler_params=pltpu.CompilerParams(collective_id=2, has_side_effects=True),
        name="gather_grads",
    )(soft, dq, own, oth, temper)


PARTS = 2


def settle_kernel(dq_in, dk_in, dv_in, temper_in, dq_ref, dk_ref, dv_ref, temper_ref, hold, in_sem, out_sem):
    rows = BLK // PARTS
    pairs = ((dq_in, dq_ref), (dk_in, dk_ref), (dv_in, dv_ref))

    def take(n):
        part = pl.ds((n % PARTS) * rows, rows)
        return pltpu.make_async_copy(pairs[n // PARTS][0].at[0, part], hold.at[n], in_sem.at[n])

    def put(n):
        part = pl.ds((n % PARTS) * rows, rows)
        return pltpu.make_async_copy(hold.at[n], pairs[n // PARTS][1].at[0, part], out_sem.at[n])

    count = 3 * PARTS
    for n in range(count):
        take(n).start()
    temper_copy = pltpu.make_async_copy(temper_in, temper_ref, in_sem.at[count])
    temper_copy.start()
    for n in range(count):
        take(n).wait()
        put(n).start()
    for n in range(count):
        put(n).wait()
    temper_copy.wait()


def settle(dq, dk, dv, temper):
    hbm = pl.BlockSpec(memory_space=pl.ANY)
    whole = jax.ShapeDtypeStruct((1, BLK, HEADS * HD), BF16)
    return pl.pallas_call(
        settle_kernel,
        out_shape=(whole, whole, whole, jax.ShapeDtypeStruct((HEADS,), F32)),
        in_specs=[hbm] * 4,
        out_specs=(hbm,) * 4,
        scratch_shapes=[
            pltpu.VMEM((3 * PARTS, BLK // PARTS, HEADS * HD), BF16),
            pltpu.SemaphoreType.DMA((3 * PARTS + 1,)),
            pltpu.SemaphoreType.DMA((3 * PARTS,)),
        ],
        name="settle",
    )(dq, dk, dv, temper)


def shards(q, k, v, g, softness, grouping, span):
    qg, kv = scatter_blocks(q, k, v, g)
    dq, own, oth, temper = attend(grouping.reshape(HEADS, BLOCKS), softness, span, qg, kv)
    return settle(*gather_grads(softness, dq, own, oth, temper))


def solution(mesh):
    tokens = P("dp", "seq", None)
    return jax.shard_map(
        shards,
        mesh=mesh,
        in_specs=(tokens, tokens, tokens, tokens, P(), P("dp", None, None, None), P()),
        out_specs=(tokens, tokens, tokens, P()),
        check_vma=False,
    )
```
